32 devices in a mesh: ctx: 8 (over z, x), head: 4 (over y, core).
Axes of the slice: x: 2, y: 2, z: 4, core: 2. Of those that a mesh axis runs over, the one named last changes fastest.
Arguments:
- x_load: bfloat16 [2048, 16384], P(('ctx', 'head')), may hold values from -6 to 6
- z_load: bfloat16 [2048, 16384], P(('ctx', 'head')), may hold values from -6 to 6
- b_load: bfloat16 [2048, 1024], P(('ctx', 'head')), may hold values from -6 to 6
- c_load: bfloat16 [2048, 1024], P(('ctx', 'head')), may hold values from -0.5 to 0.5
- dt_load: bfloat16 [2048, 128], P(('ctx', 'head')), may hold values from -3 to 3
- dt_bias: float32 [128], P('head'), may hold values from -4.5 to -3.5
- a_log: float32 [128], P('head'), may hold values from -12 to 2
- skip_gain: float32 [128], P('head'), may hold values from 0.5 to 2
- norm_gain: bfloat16 [16384], P('head'), may hold values from 0.5 to 1.5
- doc_lengths: int32 [16], replicated, may hold values from 1 to 1024, 2048 in all
- anchor: int32 [2048], P(('ctx', 'head')), may hold values from 0 to 2047, as said below
Outputs:
- mixed: bfloat16 [2048, 16384], P('ctx', 'head')
The draws below stay inside these ranges and needn't reach their ends.
Inputs may be any that keep to these rules, and one draw needn't show every extreme that they name: `anchor`: a permutation of the positions; each loader shard of 64 rows holds between 4 and 12 rows for each owner's block of 256 positions, and 12 for some owner.
All inputs are finite; a program needn't handle non-finite values.
Results may differ from the reference program's by a relative error of at most 0.0032.
Values may be sent and summed in bfloat16 or wider, within the bound.
No kernel may reach another device: no remote copies, remote signals or barrier semaphores. Data moves between devices by JAX's collectives and lax.ppermute only.
A program may use at most 192 MiB of HBM per device.

```python
import math
import jax
import jax.numpy as jnp
import numpy as np
from jax import lax

HEADS = 128
HEAD_DIM = 128
STATE = 128
GROUPS = 8
SPAN = 256
NDOCS = 16
TOK_DEV = 256
INNER = 16384
TOKENS = 2048
LOAD_ROWS = 64
MAXDOC = 1024


def draw_a_log(key, part):
    key_pick, key_fast, key_slow = jax.random.split(key, 3)
    quick = jax.random.bernoulli(key_pick, 0.5, (HEADS,))
    fast_rate = jnp.exp(jax.random.uniform(key_fast, (HEADS,), jnp.float32, jnp.log(0.7), jnp.log(5.0)))
    slow_rate = jnp.exp(jax.random.uniform(key_slow, (HEADS,), jnp.float32, jnp.log(0.1), jnp.log(1.5))) / (TOKENS * 0.02)
    return jnp.log(jnp.where(quick, fast_rate, slow_rate)).astype(jnp.float32)


def draw_anchor(key, part):
    owners = TOKENS // TOK_DEV
    loaders = TOKENS // LOAD_ROWS
    base_count = LOAD_ROWS // owners
    half_count = base_count // 2
    key_shift, key_order = jax.random.split(key)
    shifts = jax.random.permutation(key_shift, owners - 1) + 1
    source = jnp.arange(loaders, dtype=jnp.int32)[:, None]
    target = jnp.arange(owners, dtype=jnp.int32)[None, :]
    plus_one = (target == (source + shifts[0]) % owners).astype(jnp.int32)
    minus_one = (target == (source + shifts[1]) % owners).astype(jnp.int32)
    counts = base_count + half_count * (plus_one - minus_one)
    offsets = jnp.cumsum(counts, axis=0) - counts
    row_end = jnp.cumsum(counts, axis=1)
    row_begin = row_end - counts
    row_slot = jnp.arange(LOAD_ROWS, dtype=jnp.int32)
    owner_of = jnp.sum((row_end[:, None, :] <= row_slot[None, :, None]).astype(jnp.int32), axis=2)
    begin_of = jnp.take_along_axis(row_begin, owner_of, axis=1)
    offset_of = jnp.take_along_axis(offsets, owner_of, axis=1)
    position = owner_of * TOK_DEV + offset_of + row_slot[None, :] - begin_of
    order_keys = jax.random.split(key_order, loaders)
    orders = jax.vmap(lambda sub_key: jax.random.permutation(sub_key, LOAD_ROWS))(order_keys)
    shuffled = jnp.take_along_axis(position, orders, axis=1)
    return shuffled.reshape(TOKENS).astype(jnp.int32)


def levels(key, extent, cuts, low, largest):
    def one(dim, blocks):
        draws = jax.random.uniform(jax.random.fold_in(jax.random.fold_in(key, 6), dim), (blocks,), jnp.float32, low / len(cuts), largest / len(cuts))
        return jnp.repeat(jnp.exp(draws), extent[dim] // blocks).reshape((-1,) + (1,) * (len(extent) - dim - 1))

    factor_of = one(*cuts[0])
    for cut in cuts[1:]:
        factor_of = factor_of * one(*cut)
    return factor_of


def profile(amount, total, most, lean):
    portions = [(1 << 20) // math.isqrt(standing ** lean) + 1 for standing in range(2, amount + 1)]
    surplus, given = total - most - (amount - 1), [1] * (amount - 1)
    while surplus > 0:
        candidates = [i for i in range(amount - 1) if given[i] < most]
        whole, left = sum([portions[i] for i in candidates]), surplus
        for i in candidates:
            addition = min(most - given[i], max(1, left * portions[i] // whole), surplus)
            given[i] = given[i] + addition
            surplus = surplus - addition
    return np.array([most] + given)


def ragged(key, amount, total, limit, skew):
    if amount == 2:
        one = jax.random.randint(key, (), max(1, total - limit), min(limit, total - 1) + 1)
        return jnp.stack([one, total - one])
    sizes = jnp.asarray(profile(amount, total, limit, skew), jnp.int32)
    twos = (amount - 1) // 2
    giver, sink = sizes[1:1 + 2 * twos:2], sizes[2:2 + 2 * twos:2]
    margin = jnp.minimum(giver - 1, limit - sink)
    shifted = jax.random.randint(jax.random.fold_in(key, 1), (twos,), 0, 1 << 20) % (margin + 1)
    sizes = sizes.at[1:1 + 2 * twos:2].set(giver - shifted).at[2:2 + 2 * twos:2].set(sink + shifted)
    return sizes[jax.random.permutation(jax.random.fold_in(key, 2), amount)]


def normal_values(rng, shape, deviation, reach, shards=(), held_as=jnp.bfloat16):
    values = deviation * jax.random.normal(rng, shape, jnp.float32)
    if shards:
        values = values * levels(rng, shape, shards, -0.22, 0.18)
    return jnp.clip(values, -reach, reach).astype(held_as)


def setup_inputs(seed: int = 0) -> dict:
    key_list = jax.random.split(jax.random.key(seed), 12)
    x_load = normal_values(key_list[0], (TOKENS, INNER), 1.0, 6.0, ((0, 32),))
    z_load = normal_values(key_list[1], (TOKENS, INNER), 1.0, 6.0, ((0, 32),))
    b_load = normal_values(key_list[2], (TOKENS, GROUPS * STATE), 1.0, 6.0, ((0, 32),))
    c_load = normal_values(key_list[3], (TOKENS, GROUPS * STATE), STATE ** -0.5, 0.5, ((0, 32),))
    dt_load = normal_values(key_list[4], (TOKENS, HEADS), 0.5, 3.0, ((0, 32),))
    dt_bias = jnp.clip(-4.5 + 1.0 * jax.random.uniform(key_list[5], (HEADS,), jnp.float32) ** levels(key_list[5], (HEADS,), ((0, 4),), -0.2, 0.2), -4.5, -3.5)
    a_log = draw_a_log(jax.random.fold_in(key_list[11], 71), 0)
    skip_gain = jnp.clip(0.5 + 1.5 * jax.random.uniform(key_list[7], (HEADS,), jnp.float32) ** levels(key_list[7], (HEADS,), ((0, 4),), -0.2, 0.2), 0.5, 2.0)
    norm_gain = jnp.clip(1.0 + 0.1 * jax.random.normal(key_list[8], (INNER,), jnp.float32), 0.5, 1.5).astype(jnp.bfloat16)
    doc_lengths = ragged(key_list[9], NDOCS, TOKENS, MAXDOC, 2).astype(jnp.int32)
    anchor = draw_anchor(jax.random.fold_in(key_list[11], 71), 0)
    return {"x_load": x_load, "z_load": z_load, "b_load": b_load, "c_load": c_load, "dt_load": dt_load, "dt_bias": dt_bias, "a_log": a_log, "skip_gain": skip_gain, "norm_gain": norm_gain, "doc_lengths": doc_lengths, "anchor": anchor}


def doc_index(positions, starts):
    return lax.optimization_barrier(jnp.sum((starts[None, :] <= positions[:, None]).astype(jnp.int32), axis=1)) - 1

def rounded(values):
    return lax.optimization_barrier(values.astype(jnp.bfloat16)).astype(jnp.float32)

def block_parts(x_block, b_block, c_block, dt_block, log_block, doc_ids, doc_before):
    span_len = x_block.shape[0]
    head_count = x_block.shape[1]
    head_width = x_block.shape[2]
    group_count = b_block.shape[1]
    state_width = b_block.shape[2]
    per_group = head_count // group_count
    cum_log = jnp.cumsum(log_block, axis=0)
    lower_mask = jnp.arange(span_len)[:, None] >= jnp.arange(span_len)[None, :]
    keep_mask = lower_mask & (doc_ids[:, None] == doc_ids[None, :])
    cum_heads = cum_log.T
    exponent = jnp.where(keep_mask[None], cum_heads[:, :, None] - cum_heads[:, None, :], -jnp.inf)
    decay = jnp.exp(exponent)
    b_wide = b_block.astype(jnp.float32)
    c_wide = c_block.astype(jnp.float32)
    x_wide = x_block.astype(jnp.float32)
    scores = jnp.einsum('tgn,sgn->gts', c_wide, b_wide)
    scores = jnp.repeat(scores, per_group, axis=0)
    weights = rounded(scores * decay * dt_block.T[:, None, :])
    intra_part = jnp.einsum('hts,shp->thp', weights, x_wide)
    tail_weight = jnp.where((doc_ids == doc_ids[-1])[:, None], jnp.exp(cum_log[-1][None, :] - cum_log), 0.0) * dt_block
    weighted_b = rounded(b_wide[:, :, None, :] * tail_weight.reshape(span_len, group_count, per_group)[:, :, :, None])
    local_state = jnp.einsum('sgkn,sgkp->gknp', weighted_b, x_wide.reshape(span_len, group_count, per_group, head_width))
    local_state = local_state.reshape(head_count, state_width, head_width)
    entry_decay = jnp.where((doc_ids == doc_before)[:, None], jnp.exp(cum_log), 0.0)
    return (intra_part, local_state, entry_decay)

def cross_term(c_block, state_low, entry_decay):
    span_len, group_count, state_width = c_block.shape
    head_count, _, head_width = state_low.shape
    grouped = state_low.reshape(group_count, head_count // group_count, state_width, head_width)
    cross_part = jnp.einsum('tgn,gknp->tgkp', c_block.astype(jnp.float32), grouped)
    return cross_part.reshape(span_len, head_count, head_width) * entry_decay[:, :, None]

def reference(x_load, z_load, b_load, c_load, dt_load, dt_bias, a_log, skip_gain, norm_gain, doc_lengths, anchor):
    token_count = anchor.shape[0]
    inverse = jnp.zeros((token_count,), jnp.int32).at[anchor].set(jnp.arange(token_count, dtype=jnp.int32))
    starts = (jnp.cumsum(doc_lengths) - doc_lengths).astype(jnp.int32)
    decay_rate = jnp.exp(a_log)
    span_count = token_count // SPAN

    def span_step(state_in, span_index):
        row_ids = lax.dynamic_slice_in_dim(inverse, span_index * SPAN, SPAN)
        x_block = x_load[row_ids].reshape(SPAN, HEADS, HEAD_DIM)
        z_block = z_load[row_ids]
        b_block = b_load[row_ids].reshape(SPAN, GROUPS, STATE)
        c_block = c_load[row_ids].reshape(SPAN, GROUPS, STATE)
        step_size = jax.nn.softplus(dt_load[row_ids].astype(jnp.float32) + dt_bias[None, :])
        log_step = -step_size * decay_rate[None, :]
        positions = (span_index * SPAN + jnp.arange(SPAN, dtype=jnp.int32)).astype(jnp.int32)
        doc_ids = doc_index(positions, starts)
        doc_before = doc_index(positions[:1] - 1, starts)[0]
        intra_part, local_state, entry_decay = block_parts(x_block, b_block, c_block, step_size, log_step, doc_ids, doc_before)
        state_low = rounded(state_in)
        cross_part = cross_term(c_block, state_low, entry_decay)
        mixed_out = intra_part + cross_part + skip_gain[None, :, None] * x_block.astype(jnp.float32)
        gated = mixed_out.reshape(SPAN, HEADS * HEAD_DIM) * jax.nn.silu(z_block.astype(jnp.float32))
        grouped = gated.reshape(SPAN, GROUPS, -1)
        inv_rms = lax.rsqrt(lax.optimization_barrier(jnp.mean(grouped * grouped, axis=-1, keepdims=True)) + 1e-05)
        result_rows = (grouped * inv_rms).reshape(SPAN, -1) * norm_gain.astype(jnp.float32)[None, :]
        state_next = entry_decay[-1][:, None, None] * state_in + local_state
        return (state_next, result_rows.astype(jnp.bfloat16))
    initial = jnp.zeros((HEADS, STATE, HEAD_DIM), jnp.float32)
    _, outputs = lax.scan(span_step, initial, jnp.arange(span_count, dtype=jnp.int32))
    return outputs.reshape(token_count, HEADS * HEAD_DIM)
```

```python
import functools

import jax
import jax.numpy as jnp
from jax import lax
from jax.experimental import pallas as pl
from jax.experimental.pallas import tpu as pltpu
from jax.sharding import PartitionSpec as P

SPAN = 256
LANES = 128
ROWS = 8
F32 = jnp.float32
BF16 = jnp.bfloat16
BOTH = ("ctx", "head")
VMEM = pl.BlockSpec(memory_space=pltpu.VMEM)
SMEM = pl.BlockSpec(memory_space=pltpu.SMEM)
PARAMS = pltpu.CompilerParams(vmem_limit_bytes=56 * 1024 * 1024)


def iota(shape, dim):
    return lax.broadcasted_iota(jnp.int32, shape, dim)


def dot(left, right):
    return jnp.dot(left, right, preferred_element_type=F32)


def onehot(mask):
    return jnp.where(mask, 1.0, 0.0).astype(BF16)


def send_onehots(anchor, owners, block_rows, over):
    rows = anchor.shape[1]
    owner = jnp.zeros_like(anchor)
    for k in range(1, owners):
        owner = owner + jnp.where(anchor >= k * block_rows, 1, 0)
    eye = iota((rows, rows), 0) == iota((rows, rows), 1)
    owner_f = owner.astype(F32)
    owner_col = jnp.sum(jnp.where(eye, owner_f, 0.0), axis=1, keepdims=True)
    earlier = (owner_col == owner_f) & (iota((rows, rows), 0) < iota((rows, rows), 1))
    rank = jnp.sum(jnp.where(earlier, 1.0, 0.0), axis=0, keepdims=True).astype(jnp.int32)
    place = (anchor - owner * block_rows + 1).astype(F32)
    place_col = jnp.sum(jnp.where(eye, place, 0.0), axis=1, keepdims=True)
    slot = iota((owners * ROWS, rows), 0)
    first = owner * ROWS + rank
    base = onehot((slot == first) & (rank < ROWS))
    if not over:
        return base, None, None, place_col
    low = onehot((slot == first - ROWS) & (rank >= ROWS))
    high = onehot((slot == first - ROWS // 2) & (rank >= ROWS))
    return base, low, high, place_col


def pack_kernel(owners, block_rows, over, width, heads, small, anchor_ref, wide_ref, *refs):
    out_ref = refs[-1]
    base, low, high, place_col = send_onehots(anchor_ref[...], owners, block_rows, over)

    def put(column, values):
        values = values.astype(BF16).reshape(owners, ROWS, values.shape[1])
        out_ref[:, 0, :, column : column + values.shape[2]] = values

    wide = wide_ref[...]
    put(0, dot(base, wide))
    column = width
    if over:
        half = width // 2
        put(
            column,
            dot(
                jnp.concatenate([low, high], axis=1),
                jnp.concatenate([wide[:, :half], wide[:, half:]], axis=0),
            ),
        )
        column += half
    if small == 0:
        return
    b_part, c_part = refs[0][...], refs[1][...]
    if small == 1:
        put(column, dot(base, jnp.concatenate([b_part, c_part], axis=1)))
        if over:
            put(column + 2 * LANES, dot(low, b_part) + dot(high, c_part))
        return
    turn = pl.program_id(0)
    steps = refs[2][...].astype(F32)
    own = jnp.zeros_like(steps)
    lane = iota(steps.shape, 1)
    for k in range(LANES // heads):
        shifted = steps if k == 0 else pltpu.roll(steps, LANES - k * heads, 1)
        own = own + jnp.where(turn == k, shifted, 0.0)
    meta = jnp.where(lane < heads, own, jnp.where(lane == heads, place_col, 0.0)).astype(BF16)
    put(column, dot(base, jnp.concatenate([b_part, c_part, meta], axis=1)))
    if over:
        pair = dot(low, jnp.concatenate([b_part, c_part], axis=1))
        extra = dot(high, meta)
        put(column + 3 * LANES, pair + jnp.concatenate([extra, jnp.zeros_like(extra)], axis=1))


def pack(anchor, wide, smalls, part, dims, small):
    owners, columns, block_rows, over, width, heads = dims
    load_rows = wide.shape[0]
    parts = wide.shape[1] // (columns * width)
    total = width * 3 // 2 if over else width
    if small == 1:
        total += LANES * (3 if over else 2)
    if small == 2:
        total += LANES * (5 if over else 3)
    narrow = pl.BlockSpec((load_rows, LANES), lambda i: (0, i * parts + part))
    in_specs = [
        pl.BlockSpec((1, load_rows), lambda i: (0, 0)),
        pl.BlockSpec((load_rows, width), lambda i: (0, i * parts + part)),
    ]
    if small:
        in_specs += [narrow, narrow]
    if small == 2:
        in_specs += [pl.BlockSpec((load_rows, LANES), lambda i: (0, 0))]
    packed = pl.pallas_call(
        functools.partial(pack_kernel, owners, block_rows, over, width, heads, small),
        grid=(columns,),
        in_specs=in_specs,
        out_specs=pl.BlockSpec((owners, 1, ROWS, total), lambda i: (0, i, 0, 0)),
        out_shape=jax.ShapeDtypeStruct((owners, columns, ROWS, total), BF16),
        compiler_params=PARAMS,
        name=f"pack{small}",
    )(anchor, wide, *smalls)
    return packed.reshape(owners * columns, ROWS, total)


def exchange(values, axes):
    return lax.all_to_all(values, axes, split_axis=0, concat_axis=0, tiled=True)


def doc_counts(lengths_ref, positions):
    count = jnp.zeros_like(positions)
    start = jnp.int32(0)
    for k in range(lengths_ref.shape[0]):
        count = count + jnp.where(positions >= start, 1, 0)
        start = start + lengths_ref[k]
    return count


def column_of(row):
    size = row.shape[1]
    eye = iota((size, size), 0) == iota((size, size), 1)
    return jnp.sum(jnp.where(eye, row, 0.0), axis=1, keepdims=True)


def placed(q_ref, values_ref, over, start, width, stop):
    slots = values_ref.shape[0]
    own = q_ref[:, 0:slots]
    if not over:
        return dot(own, values_ref[:, start : start + width])
    half = width // 2
    extra = values_ref[:, start + stop : start + stop + half]
    first = dot(own, values_ref[:, start : start + half])
    second = dot(own, values_ref[:, start + half : start + width])
    first = first + dot(q_ref[:, slots : 2 * slots], extra)
    second = second + dot(q_ref[:, 2 * slots : 3 * slots], extra)
    return jnp.concatenate([first, second], axis=1)


def local_states(part, per_group, rows_of, tail_ref, b_placed, x_ref, entry_last, state_ref):
    b_turned = b_placed.T
    for h in range(per_group):
        head = part * per_group + h
        weighted = (b_turned * tail_ref[head : head + 1, :]).astype(BF16)
        state = dot(weighted, x_ref[:, h * LANES : (h + 1) * LANES]).astype(BF16)
        piece = min(rows_of, LANES)
        for k in range(LANES // piece):
            at = h * LANES + k * piece
            state_ref[at // rows_of, at % rows_of : at % rows_of + piece, :] = state[
                k * piece : (k + 1) * piece
            ]
    high = entry_last.astype(BF16).astype(F32)
    middle = (entry_last - high).astype(BF16).astype(F32)
    low = entry_last - high - middle
    sub = iota((ROWS, LANES), 0)
    rows = jnp.where(sub == 0, high, jnp.where(sub == 1, middle, jnp.where(sub == 2, low, 0.0)))
    for k in range(state_ref.shape[0]):
        state_ref[k, rows_of : rows_of + ROWS, :] = rows.astype(BF16)


def first_kernel(
    dims,
    place_ref,
    lengths_ref,
    arrived_ref,
    bias_ref,
    rate_ref,
    q_ref,
    x_ref,
    bc_ref,
    rows_ref,
    columns_ref,
    state_ref,
):
    owners, columns, block_rows, over, width, heads = dims
    slots = arrived_ref.shape[0]
    per_group = width // LANES
    rows_of = state_ref.shape[1] - ROWS
    column = width * 3 // 2 if over else width
    meta = arrived_ref[:, column + 2 * LANES : column + 3 * LANES]
    target = iota((block_rows, slots), 0) + 1
    spot = meta.astype(F32).T[heads : heads + 1, :].astype(jnp.int32)
    own = onehot(target == spot)
    q_ref[:, 0:slots] = own
    b_all = dot(own, arrived_ref[:, column : column + LANES])
    c_all = dot(own, arrived_ref[:, column + LANES : column + 2 * LANES])
    meta_all = dot(own, meta)
    if over:
        extra = arrived_ref[:, column + 3 * LANES : column + 4 * LANES]
        other = arrived_ref[:, column + 4 * LANES : column + 5 * LANES]
        spot = extra.astype(F32).T[heads : heads + 1, :]
        half = ROWS // 2
        inside = iota((1, slots), 1) % ROWS
        high_spot = jnp.where(inside >= half, spot, 0.0)
        low_spot = pltpu.roll(high_spot, slots - half, 1)
        low_spot = jnp.where(inside < half, low_spot, 0.0)
        low = onehot(target == low_spot.astype(jnp.int32))
        high = onehot(target == high_spot.astype(jnp.int32))
        q_ref[:, slots : 2 * slots] = low
        q_ref[:, 2 * slots : 3 * slots] = high
        b_all = b_all + dot(low, extra)
        c_all = c_all + dot(low, other)
        meta_all = meta_all + dot(high, extra)
    x_ref[...] = placed(q_ref, arrived_ref, over, 0, width, width).astype(BF16)
    bc_ref[0] = b_all.astype(BF16)
    bc_ref[1] = c_all.astype(BF16)
    raw = meta_all.T[0:heads, :] + column_of(bias_ref[...])
    small = jnp.exp(-jnp.abs(raw))
    step = jnp.maximum(raw, 0.0) + jnp.log1p(small)
    logs = -step * jnp.exp(column_of(rate_ref[...]))
    upper = jnp.where(
        iota((block_rows, block_rows), 0) <= iota((block_rows, block_rows), 1), 1.0, 0.0
    )
    cum = jnp.dot(logs, upper, preferred_element_type=F32, precision=lax.Precision.HIGHEST)
    start = place_ref[0] * block_rows
    docs = doc_counts(lengths_ref, start + iota((1, block_rows), 1))
    last = doc_counts(lengths_ref, start + block_rows - 1 + jnp.zeros((1, 1), jnp.int32))
    before = doc_counts(lengths_ref, start - 1 + jnp.zeros((1, 1), jnp.int32))
    end = cum[:, block_rows - 1 : block_rows]
    tail = jnp.where(docs == last, jnp.exp(end - cum), 0.0) * step
    entry = jnp.where(docs == before, jnp.exp(cum), 0.0)
    rows_ref[0] = step
    rows_ref[1] = cum
    rows_ref[2] = tail
    blank = jnp.zeros((LANES - heads, block_rows), F32)
    entry_turned = jnp.concatenate([entry, blank], axis=0).T
    columns_ref[0] = jnp.concatenate([cum, blank], axis=0).T
    columns_ref[1] = entry_turned
    local_states(
        0,
        per_group,
        rows_of,
        rows_ref.at[2],
        b_all,
        x_ref,
        entry_turned[block_rows - 1 : block_rows, :],
        state_ref,
    )


def later_kernel(
    dims, part, arrived_ref, q_ref, rows_ref, columns_ref, x_ref, bc_ref, state_ref
):
    owners, columns, block_rows, over, width, heads = dims
    slots = arrived_ref.shape[0]
    per_group = width // LANES
    rows_of = state_ref.shape[1] - ROWS
    column = width * 3 // 2 if over else width
    own = q_ref[:, 0:slots]
    b_all = dot(own, arrived_ref[:, column : column + LANES])
    c_all = dot(own, arrived_ref[:, column + LANES : column + 2 * LANES])
    if over:
        extra = arrived_ref[:, column + 2 * LANES : column + 3 * LANES]
        b_all = b_all + dot(q_ref[:, slots : 2 * slots], extra)
        c_all = c_all + dot(q_ref[:, 2 * slots : 3 * slots], extra)
    x_ref[...] = placed(q_ref, arrived_ref, over, 0, width, width).astype(BF16)
    bc_ref[0] = b_all.astype(BF16)
    bc_ref[1] = c_all.astype(BF16)
    local_states(
        part,
        per_group,
        rows_of,
        rows_ref.at[2],
        b_all,
        x_ref,
        columns_ref[1, block_rows - 1 : block_rows, :],
        state_ref,
    )


def intra_kernel(
    part, place_ref, lengths_ref, skip_ref, x_ref, bc_ref, rows_ref, columns_ref, y_ref
):
    block_rows, width = x_ref.shape
    per_group = width // LANES
    scores = lax.dot_general(
        bc_ref[1], bc_ref[0], (((1,), (1,)), ((), ())), preferred_element_type=F32
    )
    start = place_ref[0] * block_rows
    square = (block_rows, block_rows)
    row_docs = doc_counts(lengths_ref, start + iota((1, block_rows), 1))
    column_docs = doc_counts(lengths_ref, start + iota((block_rows, 1), 0))
    keep = (iota(square, 0) >= iota(square, 1)) & (row_docs == column_docs)
    for h in range(per_group):
        head = part * per_group + h
        across = columns_ref[0, :, head : head + 1] - rows_ref[1, head : head + 1, :]
        decay = jnp.exp(jnp.where(keep, across, -jnp.inf))
        weights = (scores * decay * rows_ref[0, head : head + 1, :]).astype(BF16)
        at = slice(h * LANES, (h + 1) * LANES)
        x_head = x_ref[:, at]
        y_ref[:, at] = dot(weights, x_head) + skip_ref[head] * x_head.astype(F32)


def scan_kernel(part, per_group, place_ref, states_ref, out_ref):
    owners, rows_of, _ = out_ref.shape
    block = min(rows_of, LANES)
    lane = iota((1, LANES), 1)
    for k in range(rows_of // block):
        at = slice(k * block, (k + 1) * block)
        head = part * per_group + (place_ref[0] * rows_of + k * block) // LANES
        state = jnp.zeros((block, LANES), F32)
        for j in range(owners):
            out_ref[j, at, :] = state.astype(BF16)
            parts = states_ref[j, rows_of : rows_of + ROWS, :].astype(F32)
            factors = parts[0:1] + parts[1:2] + parts[2:3]
            factor = jnp.sum(jnp.where(lane == head, factors, 0.0), axis=1, keepdims=True)
            state = factor * state + states_ref[j, at, :].astype(F32)


def final_kernel(
    over, part, arrived_ref, q_ref, y_ref, bc_ref, state_ref, columns_ref, gain_ref, *refs
):
    out_ref, gated_ref = refs[-2:]
    block_rows, width = y_ref.shape
    per_group = width // LANES
    gated_ref[...] = placed(q_ref, arrived_ref, over, 0, width, width)
    squares = jnp.zeros((block_rows, LANES), F32)
    for h in range(per_group):
        head = part * per_group + h
        at = slice(h * LANES, (h + 1) * LANES)
        cross = dot(bc_ref[1], state_ref[at, :])
        value = y_ref[:, at] + columns_ref[1, :, head : head + 1] * cross
        gate = gated_ref[:, at]
        value = value * (gate / (1.0 + jnp.exp(-gate)))
        gated_ref[:, at] = value
        squares = squares + value * value
    mean = jnp.sum(squares, axis=1, keepdims=True) * (1.0 / width)
    scale = lax.rsqrt(mean + 1e-05)
    for h in range(per_group):
        at = slice(h * LANES, (h + 1) * LANES)
        out_ref[:, at] = (gated_ref[:, at] * scale * gain_ref[:, at].astype(F32)).astype(BF16)


def shape(*dims, dtype=BF16):
    return jax.ShapeDtypeStruct(dims, dtype)


def body(
    x_load,
    z_load,
    b_load,
    c_load,
    dt_load,
    dt_bias,
    a_log,
    skip_gain,
    norm_gain,
    doc_lengths,
    anchor,
):
    load_rows = anchor.shape[0]
    owners = lax.axis_size("ctx")
    columns = lax.axis_size("head")
    block_rows = load_rows * columns
    capacity = 3 * load_rows // (2 * owners)
    heads = dt_bias.shape[0]
    groups = b_load.shape[1] // (columns * LANES)
    per_group = heads // groups
    width = per_group * LANES
    over = capacity > ROWS
    dims = (owners, columns, block_rows, over, width, heads)
    slots = owners * columns * ROWS
    finds = 3 if over else 1
    rows_of = width // owners
    anchor = anchor.reshape(1, load_rows)
    place = lax.axis_index("ctx").astype(jnp.int32).reshape(1)

    arrived_x = []
    arrived_z = []
    for part in range(groups):
        smalls = (b_load, c_load, dt_load) if part == 0 else (b_load, c_load)
        sent = pack(anchor, x_load, smalls, part, dims, 2 if part == 0 else 1)
        arrived_x.append(exchange(sent, BOTH).reshape(slots, sent.shape[2]))
    for part in range(groups):
        sent = pack(anchor, z_load, (), part, dims, 0)
        arrived_z.append(exchange(sent, BOTH).reshape(slots, sent.shape[2]))

    rows_x, both, partial, states = [], [], [], []
    per_part = (
        shape(block_rows, width),
        shape(2, block_rows, LANES),
    )
    state_shape = shape(owners, rows_of + ROWS, LANES)
    for part in range(groups):
        if part == 0:
            finder, row_values, both_0, rows_0, columns_0, local = pl.pallas_call(
                lambda p, l, a, b, r, q, x, bc, ro, co, st: first_kernel(
                    dims, p, l, a, b, r, q, x, bc, ro, co, st
                ),
                in_specs=[SMEM, SMEM, VMEM, VMEM, VMEM],
                out_specs=[VMEM] * 6,
                out_shape=(
                    shape(block_rows, finds * slots),
                    per_part[0],
                    per_part[1],
                    shape(3, heads, block_rows, dtype=F32),
                    shape(2, block_rows, LANES, dtype=F32),
                    state_shape,
                ),
                compiler_params=PARAMS,
                name="land_first",
            )(
                place,
                doc_lengths,
                arrived_x[0],
                dt_bias.reshape(1, heads),
                a_log.reshape(1, heads),
            )
        else:
            row_values, both_0, local = pl.pallas_call(
                functools.partial(later_kernel, dims, part),
                in_specs=[VMEM] * 4,
                out_specs=[VMEM] * 3,
                out_shape=(per_part[0], per_part[1], state_shape),
                compiler_params=PARAMS,
                name="land_later",
            )(arrived_x[part], finder, rows_0, columns_0)
        rows_x.append(row_values)
        both.append(both_0)
        gathered = exchange(local, "ctx")
        scanned = pl.pallas_call(
            functools.partial(scan_kernel, part, per_group),
            in_specs=[SMEM, VMEM],
            out_specs=VMEM,
            out_shape=shape(owners, rows_of, LANES),
            compiler_params=PARAMS,
            name="scan",
        )(place, gathered)
        states.append(exchange(scanned, "ctx").reshape(width, LANES))
        partial.append(
            pl.pallas_call(
                functools.partial(intra_kernel, part),
                in_specs=[SMEM, SMEM, SMEM, VMEM, VMEM, VMEM, VMEM],
                out_specs=VMEM,
                out_shape=shape(block_rows, width, dtype=F32),
                compiler_params=PARAMS,
                name="intra",
            )(place, doc_lengths, skip_gain, row_values, both_0, rows_0, columns_0)
        )

    result = None
    gain = norm_gain.reshape(1, groups * width)
    for part in range(groups):
        whole = pl.BlockSpec(memory_space=pltpu.VMEM)
        operands = [arrived_z[part], finder, partial[part], both[part], states[part], columns_0, gain]
        full = lambda a: pl.BlockSpec(a.shape, lambda i, n=a.ndim: (0,) * n)
        in_specs = [full(a) for a in operands[:-1]]
        in_specs.append(pl.BlockSpec((1, width), lambda i, part=part: (0, part)))
        aliases = {}
        if result is not None:
            aliases = {len(operands): 0}
            operands.append(result)
            in_specs.append(pl.BlockSpec(memory_space=pl.ANY))
        result = pl.pallas_call(
            functools.partial(final_kernel, over, part),
            grid=(1,),
            in_specs=in_specs,
            out_specs=pl.BlockSpec((block_rows, width), lambda i, part=part: (0, part)),
            out_shape=shape(block_rows, groups * width),
            scratch_shapes=[pltpu.VMEM((block_rows, width), F32)],
            input_output_aliases=aliases,
            compiler_params=PARAMS,
            name="final",
        )(*operands)
    return result


def solution(mesh):
    in_specs = (
        P(BOTH, None),
        P(BOTH, None),
        P(BOTH, None),
        P(BOTH, None),
        P(BOTH, None),
        P("head"),
        P("head"),
        P("head"),
        P("head"),
        P(),
        P(BOTH),
    )
    out_specs = P("ctx", "head")
    return jax.shard_map(body, mesh=mesh, in_specs=in_specs, out_specs=out_specs, check_vma=False)
```

```python
import functools

import jax
import jax.numpy as jnp
from jax import lax
from jax.experimental import pallas as pl
from jax.experimental.pallas import tpu as pltpu
from jax.sharding import PartitionSpec as P

LANES = 128
ROWS = 8
F32 = jnp.float32
BF16 = jnp.bfloat16
BOTH = ("ctx", "head")
VMEM = pl.BlockSpec(memory_space=pltpu.VMEM)
SMEM = pl.BlockSpec(memory_space=pltpu.SMEM)
PARAMS = pltpu.CompilerParams(vmem_limit_bytes=56 * 1024 * 1024)


def iota(shape, dim):
    return lax.broadcasted_iota(jnp.int32, shape, dim)


def dot(left, right):
    return jnp.dot(left, right, preferred_element_type=F32)


def onehot(mask):
    return jnp.where(mask, 1.0, 0.0).astype(BF16)


def send_onehots(anchor, owners, block_rows, over):
    rows = anchor.shape[1]
    owner = jnp.zeros_like(anchor)
    for k in range(1, owners):
        owner = owner + jnp.where(anchor >= k * block_rows, 1, 0)
    eye = iota((rows, rows), 0) == iota((rows, rows), 1)
    owner_f = owner.astype(F32)
    owner_col = jnp.sum(jnp.where(eye, owner_f, 0.0), axis=1, keepdims=True)
    earlier = (owner_col == owner_f) & (iota((rows, rows), 0) < iota((rows, rows), 1))
    rank = jnp.sum(jnp.where(earlier, 1.0, 0.0), axis=0, keepdims=True).astype(jnp.int32)
    place = (anchor - owner * block_rows + 1).astype(F32)
    place_col = jnp.sum(jnp.where(eye, place, 0.0), axis=1, keepdims=True)
    slot = iota((owners * ROWS, rows), 0)
    first = owner * ROWS + rank
    base = onehot((slot == first) & (rank < ROWS))
    if not over:
        return base, None, None, place_col
    low = onehot((slot == first - ROWS) & (rank >= ROWS))
    high = onehot((slot == first - ROWS // 2) & (rank >= ROWS))
    return base, low, high, place_col


def pack_kernel(owners, block_rows, over, width, heads, small, anchor_ref, wide_ref, *refs):
    out_ref = refs[-1]
    base, low, high, place_col = send_onehots(anchor_ref[...], owners, block_rows, over)

    def put(column, values):
        values = values.astype(BF16).reshape(owners, ROWS, values.shape[1])
        out_ref[:, 0, :, column : column + values.shape[2]] = values

    wide = wide_ref[...]
    put(0, dot(base, wide))
    column = width
    if over:
        half = width // 2
        put(
            column,
            dot(
                jnp.concatenate([low, high], axis=1),
                jnp.concatenate([wide[:, :half], wide[:, half:]], axis=0),
            ),
        )
        column += half
    if small == 0:
        return
    b_part, c_part = refs[0][...], refs[1][...]
    if small == 1:
        put(column, dot(base, jnp.concatenate([b_part, c_part], axis=1)))
        if over:
            put(column + 2 * LANES, dot(low, b_part) + dot(high, c_part))
        return
    turn = pl.program_id(0)
    steps = refs[2][...].astype(F32)
    own = jnp.zeros_like(steps)
    lane = iota(steps.shape, 1)
    for k in range(LANES // heads):
        shifted = steps if k == 0 else pltpu.roll(steps, LANES - k * heads, 1)
        own = own + jnp.where(turn == k, shifted, 0.0)
    meta = jnp.where(lane < heads, own, jnp.where(lane == heads, place_col, 0.0)).astype(BF16)
    put(column, dot(base, jnp.concatenate([b_part, c_part, meta], axis=1)))
    if over:
        pair = dot(low, jnp.concatenate([b_part, c_part], axis=1))
        extra = dot(high, meta)
        put(column + 3 * LANES, pair + jnp.concatenate([extra, jnp.zeros_like(extra)], axis=1))


def pack(anchor, wide, smalls, part, dims, small):
    owners, columns, block_rows, over, width, heads = dims
    load_rows = wide.shape[0]
    parts = wide.shape[1] // (columns * width)
    total = width * 3 // 2 if over else width
    if small == 1:
        total += LANES * (3 if over else 2)
    if small == 2:
        total += LANES * (5 if over else 3)
    count = parts if part is None else 1
    group = (lambda i, k: i * parts + k) if part is None else (lambda i, k: i * parts + part)
    narrow = pl.BlockSpec((load_rows, LANES), lambda i, k: (0, group(i, k)))
    in_specs = [
        pl.BlockSpec((1, load_rows), lambda i, k: (0, 0)),
        pl.BlockSpec((load_rows, width), lambda i, k: (0, group(i, k))),
    ]
    if small:
        in_specs += [narrow, narrow]
    if small == 2:
        in_specs += [pl.BlockSpec((load_rows, LANES), lambda i, k: (0, 0))]
    packed = pl.pallas_call(
        functools.partial(pack_kernel, owners, block_rows, over, width, heads, small),
        grid=(columns, count),
        in_specs=in_specs,
        out_specs=pl.BlockSpec((owners, 1, ROWS, total), lambda i, k: (0, i, 0, k)),
        out_shape=jax.ShapeDtypeStruct((owners, columns, ROWS, total * count), BF16),
        compiler_params=PARAMS,
    )(anchor, wide, *smalls)
    return packed.reshape(owners * columns, ROWS, total * count)


def exchange(values, axes):
    return lax.all_to_all(values, axes, split_axis=0, concat_axis=0, tiled=True)


def doc_counts(lengths_ref, positions):
    count = jnp.zeros_like(positions)
    start = jnp.int32(0)
    for k in range(lengths_ref.shape[0]):
        count = count + jnp.where(positions >= start, 1, 0)
        start = start + lengths_ref[k]
    return count


def column_of(row):
    size = row.shape[1]
    eye = iota((size, size), 0) == iota((size, size), 1)
    return jnp.sum(jnp.where(eye, row, 0.0), axis=1, keepdims=True)


def placed(q_ref, values_ref, over, start, width, stop):
    slots = values_ref.shape[0]
    own = q_ref[:, 0:slots]
    if not over:
        return dot(own, values_ref[:, start : start + width])
    half = width // 2
    extra = values_ref[:, start + stop : start + stop + half]
    first = dot(own, values_ref[:, start : start + half])
    second = dot(own, values_ref[:, start + half : start + width])
    first = first + dot(q_ref[:, slots : 2 * slots], extra)
    second = second + dot(q_ref[:, 2 * slots : 3 * slots], extra)
    return jnp.concatenate([first, second], axis=1)


def local_states(part, per_group, tail_ref, b_placed, x_ref, entry_last, state_ref):
    b_turned = b_placed.T
    for h in range(per_group):
        head = part * per_group + h
        weighted = (b_turned * tail_ref[head : head + 1, :]).astype(BF16)
        at = slice(h * LANES, (h + 1) * LANES)
        state_ref[at, :] = dot(weighted, x_ref[:, at]).astype(BF16)
    high = entry_last.astype(BF16).astype(F32)
    middle = (entry_last - high).astype(BF16).astype(F32)
    low = entry_last - high - middle
    sub = iota((ROWS, LANES), 0)
    rows = jnp.where(sub == 0, high, jnp.where(sub == 1, middle, jnp.where(sub == 2, low, 0.0)))
    state_ref[per_group * LANES :, :] = rows.astype(BF16)


def first_kernel(
    dims,
    place_ref,
    lengths_ref,
    arrived_ref,
    bias_ref,
    rate_ref,
    q_ref,
    x_ref,
    bc_ref,
    rows_ref,
    columns_ref,
    state_ref,
):
    _, _, block_rows, over, width, heads = dims
    slots = arrived_ref.shape[0]
    per_group = width // LANES
    column = width * 3 // 2 if over else width
    meta = arrived_ref[:, column + 2 * LANES : column + 3 * LANES]
    target = iota((block_rows, slots), 0) + 1
    spot = meta.astype(F32).T[heads : heads + 1, :].astype(jnp.int32)
    own = onehot(target == spot)
    q_ref[:, 0:slots] = own
    b_all = dot(own, arrived_ref[:, column : column + LANES])
    c_all = dot(own, arrived_ref[:, column + LANES : column + 2 * LANES])
    meta_all = dot(own, meta)
    if over:
        extra = arrived_ref[:, column + 3 * LANES : column + 4 * LANES]
        other = arrived_ref[:, column + 4 * LANES : column + 5 * LANES]
        spot = extra.astype(F32).T[heads : heads + 1, :]
        half = ROWS // 2
        inside = iota((1, slots), 1) % ROWS
        high_spot = jnp.where(inside >= half, spot, 0.0)
        low_spot = pltpu.roll(high_spot, slots - half, 1)
        low_spot = jnp.where(inside < half, low_spot, 0.0)
        low = onehot(target == low_spot.astype(jnp.int32))
        high = onehot(target == high_spot.astype(jnp.int32))
        q_ref[:, slots : 2 * slots] = low
        q_ref[:, 2 * slots : 3 * slots] = high
        b_all = b_all + dot(low, extra)
        c_all = c_all + dot(low, other)
        meta_all = meta_all + dot(high, extra)
    x_ref[...] = placed(q_ref, arrived_ref, over, 0, width, width).astype(BF16)
    bc_ref[0] = b_all.astype(BF16)
    bc_ref[1] = c_all.astype(BF16)
    raw = meta_all.T[0:heads, :] + column_of(bias_ref[...])
    small = jnp.exp(-jnp.abs(raw))
    step = jnp.maximum(raw, 0.0) + jnp.log1p(small)
    logs = -step * jnp.exp(column_of(rate_ref[...]))
    upper = jnp.where(
        iota((block_rows, block_rows), 0) <= iota((block_rows, block_rows), 1), 1.0, 0.0
    )
    cum = jnp.dot(logs, upper, preferred_element_type=F32, precision=lax.Precision.HIGHEST)
    start = place_ref[0] * block_rows
    docs = doc_counts(lengths_ref, start + iota((1, block_rows), 1))
    last = doc_counts(lengths_ref, start + block_rows - 1 + jnp.zeros((1, 1), jnp.int32))
    before = doc_counts(lengths_ref, start - 1 + jnp.zeros((1, 1), jnp.int32))
    end = cum[:, block_rows - 1 : block_rows]
    tail = jnp.where(docs == last, jnp.exp(end - cum), 0.0) * step
    entry = jnp.where(docs == before, jnp.exp(cum), 0.0)
    rows_ref[0] = step
    rows_ref[1] = cum
    rows_ref[2] = tail
    blank = jnp.zeros((LANES - heads, block_rows), F32)
    entry_turned = jnp.concatenate([entry, blank], axis=0).T
    columns_ref[0] = jnp.concatenate([cum, blank], axis=0).T
    columns_ref[1] = entry_turned
    local_states(
        0,
        per_group,
        rows_ref.at[2],
        b_all,
        x_ref,
        entry_turned[block_rows - 1 : block_rows, :],
        state_ref,
    )


def later_kernel(
    dims, part, arrived_ref, q_ref, rows_ref, columns_ref, x_ref, bc_ref, state_ref
):
    _, _, block_rows, over, width, _ = dims
    slots = arrived_ref.shape[0]
    per_group = width // LANES
    column = width * 3 // 2 if over else width
    own = q_ref[:, 0:slots]
    b_all = dot(own, arrived_ref[:, column : column + LANES])
    c_all = dot(own, arrived_ref[:, column + LANES : column + 2 * LANES])
    if over:
        extra = arrived_ref[:, column + 2 * LANES : column + 3 * LANES]
        b_all = b_all + dot(q_ref[:, slots : 2 * slots], extra)
        c_all = c_all + dot(q_ref[:, 2 * slots : 3 * slots], extra)
    x_ref[...] = placed(q_ref, arrived_ref, over, 0, width, width).astype(BF16)
    bc_ref[0] = b_all.astype(BF16)
    bc_ref[1] = c_all.astype(BF16)
    local_states(
        part,
        per_group,
        rows_ref.at[2],
        b_all,
        x_ref,
        columns_ref[1, block_rows - 1 : block_rows, :],
        state_ref,
    )


def intra_kernel(
    part, place_ref, lengths_ref, skip_ref, x_ref, bc_ref, rows_ref, columns_ref, y_ref
):
    block_rows, width = x_ref.shape
    per_group = width // LANES
    scores = lax.dot_general(
        bc_ref[1], bc_ref[0], (((1,), (1,)), ((), ())), preferred_element_type=F32
    )
    start = place_ref[0] * block_rows
    square = (block_rows, block_rows)
    row_docs = doc_counts(lengths_ref, start + iota((1, block_rows), 1))
    column_docs = doc_counts(lengths_ref, start + iota((block_rows, 1), 0))
    keep = (iota(square, 0) >= iota(square, 1)) & (row_docs == column_docs)
    for h in range(per_group):
        head = part * per_group + h
        across = columns_ref[0, :, head : head + 1] - rows_ref[1, head : head + 1, :]
        decay = jnp.exp(jnp.where(keep, across, -jnp.inf))
        weights = (scores * decay * rows_ref[0, head : head + 1, :]).astype(BF16)
        at = slice(h * LANES, (h + 1) * LANES)
        x_head = x_ref[:, at]
        y_ref[:, at] = dot(weights, x_head) + skip_ref[head] * x_head.astype(F32)


def decays(rows):
    parts = rows.astype(F32)
    return parts[0:1] + parts[1:2] + parts[2:3]


def one_lane(row, index):
    return jnp.sum(jnp.where(iota((1, LANES), 1) == index, row, 0.0), axis=1, keepdims=True)


def offer_kernel(place_ref, state_ref, send_ref):
    half = send_ref.shape[0] - ROWS
    side = place_ref[0] % 2
    send_ref[0:half, :] = jnp.where(side == 0, state_ref[half : 2 * half], state_ref[0:half])
    send_ref[half:, :] = state_ref[2 * half :, :]


def meet_kernel(part, place_ref, state_ref, got_ref, total_ref, sent_ref, decay_ref):
    half = got_ref.shape[0] - ROWS
    side = place_ref[0] % 2
    own = decays(state_ref[2 * half :, :])
    other = decays(got_ref[half:, :])
    decay_ref[...] = jnp.broadcast_to(own * other, decay_ref.shape)
    second = jnp.where(side == 0, other, own)
    for q in range(half // LANES):
        at = slice(q * LANES, (q + 1) * LANES)
        below = slice(half + q * LANES, half + (q + 1) * LANES)
        kept = jnp.where(side == 0, state_ref[at, :], state_ref[below, :]).astype(F32)
        got = got_ref[at, :].astype(F32)
        index = (2 * part + side) * (half // LANES) + q
        fresh = jnp.where(side == 0, got, kept)
        total = one_lane(second, index) * jnp.where(side == 0, kept, got) + fresh
        total_ref[at, :] = total
        sent_ref[at, :] = total.astype(BF16)


def step_kernel(part, place_ref, total_ref, decay_ref, got_ref, sent_ref):
    half = got_ref.shape[0]
    side = place_ref[0] % 2
    for q in range(half // LANES):
        at = slice(q * LANES, (q + 1) * LANES)
        index = (2 * part + side) * (half // LANES) + q
        decay = one_lane(decay_ref[0:1, :], index)
        sent_ref[at, :] = (decay * got_ref[at, :].astype(F32) + total_ref[at, :]).astype(BF16)


def split_kernel(part, place_ref, state_ref, got_ref, *refs):
    keep_ref, send_ref = refs[-2:]
    half = got_ref.shape[0] - ROWS
    side = place_ref[0] % 2
    first = jnp.where(side == 0, decays(state_ref[2 * half :, :]), decays(got_ref[half:, :]))
    for q in range(half // LANES):
        at = slice(q * LANES, (q + 1) * LANES)
        index = (2 * part + side) * (half // LANES) + q
        entering = refs[0][at, :].astype(F32)
        for ref in refs[1:-2]:
            entering = entering + ref[at, :].astype(F32)
        earlier = jnp.where(side == 0, state_ref[at, :], got_ref[at, :]).astype(F32)
        after = one_lane(first, index) * entering + earlier
        keep_ref[at, :] = jnp.where(side == 0, entering, after).astype(BF16)
        send_ref[at, :] = jnp.where(side == 0, after, entering).astype(BF16)


def enter(part, place, state):
    blocks = lax.axis_size("ctx")
    half = (state.shape[0] - ROWS) // 2
    pairs = [(i, i ^ 1) for i in range(blocks)]
    call = functools.partial(pl.pallas_call, compiler_params=PARAMS)
    shared = dict(out_specs=VMEM, out_shape=shape(half, LANES))
    offered = call(
        offer_kernel,
        in_specs=[SMEM, VMEM],
        out_specs=VMEM,
        out_shape=shape(half + ROWS, LANES),
        name="offer",
    )(place, state)
    got = lax.ppermute(offered, "ctx", pairs)
    total, sent, decay = call(
        functools.partial(meet_kernel, part),
        in_specs=[SMEM, VMEM, VMEM],
        out_specs=[VMEM] * 3,
        out_shape=(
            shape(half, LANES, dtype=F32),
            shape(half, LANES),
            shape(ROWS, LANES, dtype=F32),
        ),
        name="meet",
    )(place, state, got)
    received = []
    for k in range(blocks // 2 - 1):
        if k > 0:
            sent = call(
                functools.partial(step_kernel, part),
                in_specs=[SMEM, VMEM, VMEM, VMEM],
                name="step",
                **shared,
            )(place, total, decay, received[-1])
        hops = [(2 * k + side, 2 * k + 2 + side) for side in range(2)]
        received.append(lax.ppermute(sent, "ctx", hops))
    keep, send = call(
      functools.partial(split_kernel, part),
      in_specs=[SMEM] + [VMEM] * (2 + len(received)),
      out_specs=[VMEM] * 2,
      out_shape=(shape(half, LANES),) * 2,
      name="split",
    )(place, state, got, *received)
    return keep, lax.ppermute(send, "ctx", pairs)


def final_kernel(over, groups, place_ref, arrived_ref, q_ref, columns_ref, gain_ref, *refs):
    out_ref, gated_ref = refs[-2:]
    block_rows = out_ref.shape[0]
    width = out_ref.shape[1] // groups
    per_group = width // LANES
    stride = arrived_ref.shape[1] // groups
    side = place_ref[0] % 2
    for part in range(groups):
        y_ref, bc_ref, keep_ref, got_ref = refs[4 * part : 4 * part + 4]
        gated_ref[...] = placed(q_ref, arrived_ref.at[:, part * stride : (part + 1) * stride], over, 0, width, width)
        c_rows = bc_ref[0]
        squares = jnp.zeros((block_rows, LANES), F32)
        for h in range(per_group):
            head = part * per_group + h
            at = slice(h * LANES, (h + 1) * LANES)
            low = h < per_group // 2
            of = slice((h % (per_group // 2)) * LANES, (h % (per_group // 2) + 1) * LANES)
            state = jnp.where((side == 0) == low, keep_ref[of, :], got_ref[of, :])
            cross = dot(c_rows, state)
            value = y_ref[:, at] + columns_ref[0, :, head : head + 1] * cross
            gate = 0.5 * gated_ref[:, at]
            value = value * (gate * jnp.tanh(gate) + gate)
            gated_ref[:, at] = value
            squares = squares + value * value
        mean = jnp.sum(squares, axis=1, keepdims=True) * (1.0 / width)
        scale = lax.rsqrt(mean + 1e-05)
        for h in range(per_group):
            at = slice(h * LANES, (h + 1) * LANES)
            to = slice((part * per_group + h) * LANES, (part * per_group + h + 1) * LANES)
            out_ref[:, to] = (gated_ref[:, at] * scale * gain_ref[:, to].astype(F32)).astype(BF16)


def shape(*dims, dtype=BF16):
    return jax.ShapeDtypeStruct(dims, dtype)


def body(
    x_load,
    z_load,
    b_load,
    c_load,
    dt_load,
    dt_bias,
    a_log,
    skip_gain,
    norm_gain,
    doc_lengths,
    anchor,
):
    load_rows = anchor.shape[0]
    owners = lax.axis_size("ctx")
    columns = lax.axis_size("head")
    block_rows = load_rows * columns
    capacity = 3 * load_rows // (2 * owners)
    heads = dt_bias.shape[0]
    groups = b_load.shape[1] // (columns * LANES)
    per_group = heads // groups
    width = per_group * LANES
    over = capacity > ROWS
    dims = (owners, columns, block_rows, over, width, heads)
    slots = owners * columns * ROWS
    finds = 3 if over else 1
    anchor = anchor.reshape(1, load_rows)
    place = lax.axis_index("ctx").astype(jnp.int32).reshape(1)

    arrived_x = []
    for part in range(groups):
        smalls = (b_load, c_load, dt_load) if part == 0 else (b_load, c_load)
        sent = pack(anchor, x_load, smalls, part, dims, 2 if part == 0 else 1)
        arrived_x.append(exchange(sent, BOTH).reshape(slots, sent.shape[2]))
    sent = pack(anchor, z_load, (), None, dims, 0)
    arrived_z = exchange(sent, BOTH).reshape(slots, sent.shape[2])

    finals = []
    per_part = (
        shape(block_rows, width),
        shape(2, block_rows, LANES),
    )
    state_shape = shape(width + ROWS, LANES)
    for part in range(groups):
        if part == 0:
            finder, row_values, both, rows_0, columns_0, local = pl.pallas_call(
                functools.partial(first_kernel, dims),
                in_specs=[SMEM, SMEM, VMEM, VMEM, VMEM],
                out_specs=[VMEM] * 6,
                out_shape=(
                    shape(block_rows, finds * slots),
                    per_part[0],
                    per_part[1],
                    shape(3, heads, block_rows, dtype=F32),
                    shape(2, block_rows, LANES, dtype=F32),
                    state_shape,
                ),
                compiler_params=PARAMS,
                name="land_first",
            )(place, doc_lengths, arrived_x[0], dt_bias.reshape(1, heads), a_log.reshape(1, heads))
        else:
            row_values, both, local = pl.pallas_call(
                functools.partial(later_kernel, dims, part),
                in_specs=[VMEM] * 4,
                out_specs=[VMEM] * 3,
                out_shape=(per_part[0], per_part[1], state_shape),
                compiler_params=PARAMS,
                name="land_later",
            )(arrived_x[part], finder, rows_0, columns_0)
        keep, got = enter(part, place, local)
        partial = pl.pallas_call(
            functools.partial(intra_kernel, part),
            in_specs=[SMEM, SMEM, SMEM, VMEM, VMEM, VMEM, VMEM],
            out_specs=VMEM,
            out_shape=shape(block_rows, width, dtype=F32),
            compiler_params=PARAMS,
            name="intra",
        )(place, doc_lengths, skip_gain, row_values, both, rows_0, columns_0)
        finals += [partial, both, keep, got]

    tile = block_rows // 4
    full = lambda a: pl.BlockSpec(a.shape, lambda i, n=a.ndim: (0,) * n)
    gain = norm_gain.reshape(1, groups * width)
    in_specs = [
        SMEM,
        full(arrived_z),
        pl.BlockSpec((tile, finds * slots), lambda i: (i, 0)),
        pl.BlockSpec((1, tile, LANES), lambda i: (1, i, 0)),
        full(gain),
    ]
    for part in range(groups):
        keep = finals[4 * part + 2]
        in_specs += [
            pl.BlockSpec((tile, width), lambda i: (i, 0)),
            pl.BlockSpec((1, tile, LANES), lambda i: (1, i, 0)),
            full(keep),
            full(keep),
        ]
    return pl.pallas_call(
        functools.partial(final_kernel, over, groups),
        grid=(block_rows // tile,),
        in_specs=in_specs,
        out_specs=pl.BlockSpec((tile, groups * width), lambda i: (i, 0)),
        out_shape=shape(block_rows, groups * width),
        scratch_shapes=[pltpu.VMEM((tile, width), F32)],
        compiler_params=PARAMS,
        name="final",
    )(place, arrived_z, finder, columns_0, gain, *finals)


def solution(mesh):
    in_specs = (
        P(BOTH, None),
        P(BOTH, None),
        P(BOTH, None),
        P(BOTH, None),
        P(BOTH, None),
        P("head"),
        P("head"),
        P("head"),
        P("head"),
        P(),
        P(BOTH),
    )
    out_specs = P("ctx", "head")

    return jax.shard_map(body, mesh=mesh, in_specs=in_specs, out_specs=out_specs, check_vma=False)
```

```python
import functools

import jax
import jax.numpy as jnp
from jax import lax
from jax.experimental import pallas as pl
from jax.experimental.pallas import tpu as pltpu
from jax.sharding import PartitionSpec as P

LANES = 128
ROWS = 8
F32 = jnp.float32
BF16 = jnp.bfloat16
BOTH = ("ctx", "head")
VMEM = pl.BlockSpec(memory_space=pltpu.VMEM)
SMEM = pl.BlockSpec(memory_space=pltpu.SMEM)
PARAMS = pltpu.CompilerParams(vmem_limit_bytes=56 * 1024 * 1024)


def iota(shape, dim):
    return lax.broadcasted_iota(jnp.int32, shape, dim)


def dot(left, right):
    return jnp.dot(left, right, preferred_element_type=F32)


def onehot(mask):
    return jnp.where(mask, 1.0, 0.0).astype(BF16)


def send_onehots(anchor, owners, block_rows, over):
    rows = anchor.shape[1]
    owner = jnp.zeros_like(anchor)
    for k in range(1, owners):
        owner = owner + jnp.where(anchor >= k * block_rows, 1, 0)
    eye = iota((rows, rows), 0) == iota((rows, rows), 1)
    owner_f = owner.astype(F32)
    owner_col = jnp.sum(jnp.where(eye, owner_f, 0.0), axis=1, keepdims=True)
    earlier = (owner_col == owner_f) & (iota((rows, rows), 0) < iota((rows, rows), 1))
    rank = jnp.sum(jnp.where(earlier, 1.0, 0.0), axis=0, keepdims=True).astype(jnp.int32)
    place = (anchor - owner * block_rows + 1).astype(F32)
    place_col = jnp.sum(jnp.where(eye, place, 0.0), axis=1, keepdims=True)
    slot = iota((owners * ROWS, rows), 0)
    first = owner * ROWS + rank
    base = onehot((slot == first) & (rank < ROWS))
    if not over:
        return base, None, None, place_col
    low = onehot((slot == first - ROWS) & (rank >= ROWS))
    high = onehot((slot == first - ROWS // 2) & (rank >= ROWS))
    return base, low, high, place_col


def pack_kernel(dims, small, anchor_ref, wide_ref, *refs):
    owners, _, block_rows, over, groups, width, heads = dims
    out_ref, base_ref, extra_ref, place_ref = refs[-4:]
    load_rows = wide_ref.shape[0]

    @pl.when(pl.program_id(0) == 0)
    def _():
        base, low, high, place_col = send_onehots(anchor_ref[...], owners, block_rows, over)
        base_ref[...] = base
        place_ref[...] = jnp.broadcast_to(place_col, place_ref.shape)
        if over:
            extra_ref[:, 0:load_rows] = low
            extra_ref[:, load_rows:] = high

    def put(column, values):
        values = values.astype(BF16).reshape(owners, ROWS, values.shape[1])
        out_ref[:, 0, :, column : column + values.shape[2]] = values

    def folded(low, high):
        return dot(extra_ref[...], jnp.concatenate([low, high], axis=0))

    column = 0
    for part in range(groups):
        at = part * width
        put(column, dot(base_ref[...], wide_ref[:, at : at + width]))
        column += width
        if over:
            half = width // 2
            put(column, folded(wide_ref[:, at : at + half], wide_ref[:, at + half : at + width]))
            column += half
    if not small:
        return
    b_part, c_part, dt_part = refs[0][...], refs[1][...], refs[2][...]
    steps = dt_part.astype(F32)
    own = jnp.zeros_like(steps)
    lane = iota(steps.shape, 1)
    for k in range(LANES // heads):
        shifted = steps if k == 0 else pltpu.roll(steps, LANES - k * heads, 1)
        own = own + jnp.where(pl.program_id(0) == k, shifted, 0.0)
    meta = jnp.where(lane < heads, own, jnp.where(lane == heads, place_ref[...], 0.0))
    put(column, dot(base_ref[...], jnp.concatenate([b_part, c_part], axis=1)))
    column += 2 * b_part.shape[1]
    tile = dot(base_ref[...], meta.astype(BF16))
    if over:
        turned = pltpu.roll(meta, LANES // 2, 1).astype(BF16)
        tile = tile + dot(extra_ref[:, 0:load_rows], turned)
    put(column, tile)
    if over:
        put(column + LANES, folded(b_part, c_part))


def pack(anchor, wide, smalls, dims):
    owners, columns, _, over, groups, width, _ = dims
    load_rows = wide.shape[0]
    total = groups * (width * 3 // 2 if over else width)
    if smalls:
        total += LANES * (groups * (3 if over else 2) + 1)
    in_specs = [
        pl.BlockSpec((1, load_rows), lambda i: (0, 0)),
        pl.BlockSpec((load_rows, groups * width), lambda i: (0, i)),
    ]
    if smalls:
        in_specs += [pl.BlockSpec((load_rows, groups * LANES), lambda i: (0, i))] * 2
        in_specs += [pl.BlockSpec((load_rows, LANES), lambda i: (0, 0))]
    packed = pl.pallas_call(
        functools.partial(pack_kernel, dims, bool(smalls)),
        grid=(columns,),
        in_specs=in_specs,
        out_specs=pl.BlockSpec((owners, 1, ROWS, total), lambda i: (0, i, 0, 0)),
        out_shape=shape(owners, columns, ROWS, total),
        scratch_shapes=[
            pltpu.VMEM((owners * ROWS, load_rows), BF16),
            pltpu.VMEM((owners * ROWS, 2 * load_rows), BF16),
            pltpu.VMEM((load_rows, LANES), F32),
        ],
        compiler_params=PARAMS,
        name="pack",
    )(anchor, wide, *smalls)
    return packed.reshape(owners * columns, ROWS, total)


def exchange(values, axes):
    return lax.all_to_all(values, axes, split_axis=0, concat_axis=0, tiled=True)


def doc_counts(lengths_ref, positions):
    count = jnp.zeros_like(positions)
    start = jnp.int32(0)
    for k in range(lengths_ref.shape[0]):
        count = count + jnp.where(positions >= start, 1, 0)
        start = start + lengths_ref[k]
    return count


def column_of(row):
    size = row.shape[1]
    eye = iota((size, size), 0) == iota((size, size), 1)
    return jnp.sum(jnp.where(eye, row, 0.0), axis=1, keepdims=True)


def placed(q_ref, values_ref, over, width):
    slots = values_ref.shape[0]
    half = width // 2
    if not over:
        return dot(q_ref[...], values_ref[:, 0:half]), dot(q_ref[...], values_ref[:, half:width])
    extra = values_ref[:, width : width + half]
    first = jnp.concatenate([extra, values_ref[:, 0:half]], axis=0)
    second = jnp.concatenate([values_ref[:, half:width], extra], axis=0)
    return dot(q_ref[:, 0 : 2 * slots], first), dot(q_ref[:, slots : 3 * slots], second)


def land(dims, part, side, q_ref, wide_ref, small_ref, rows_ref, decay_ref, refs):
    _, _, _, over, groups, width, _ = dims
    x_ref, bc_ref, keep_ref, offer_ref = refs
    slots = wide_ref.shape[0]
    per_group = width // LANES
    b_slots = small_ref[:, part * LANES : (part + 1) * LANES]
    c_slots = small_ref[:, (groups + part) * LANES : (groups + part + 1) * LANES]
    if over:
        at = (2 * groups + 1 + part) * LANES
        extra = small_ref[:, at : at + LANES]
        b_all = dot(q_ref[:, 0 : 2 * slots], jnp.concatenate([extra, b_slots], axis=0))
        c_all = dot(q_ref[:, slots : 3 * slots], jnp.concatenate([c_slots, extra], axis=0))
    else:
        b_all = dot(q_ref[...], b_slots)
        c_all = dot(q_ref[...], c_slots)
    bc_ref[0] = b_all.astype(BF16)
    bc_ref[1] = c_all.astype(BF16)
    first, second = placed(q_ref, wide_ref, over, width)
    x_ref[:, 0 : width // 2] = first.astype(BF16)
    x_ref[:, width // 2 :] = second.astype(BF16)
    b_turned = b_all.T

    def state_of(h):
        head = part * per_group + h
        weighted = (b_turned * rows_ref[2, head : head + 1, :]).astype(BF16)
        return dot(weighted, x_ref[:, h * LANES : (h + 1) * LANES])

    half = per_group // 2
    for q in range(half):
        low, high = state_of(q), state_of(half + q)
        at = slice(q * LANES, (q + 1) * LANES)
        keep_ref[at, :] = jnp.where(side == 0, low, high).astype(BF16)
        offer_ref[at, :] = jnp.where(side == 0, high, low).astype(BF16)
    decay = decay_ref[part * per_group : (part + 1) * per_group, :]
    top = decay.astype(BF16).astype(F32)
    middle = (decay - top).astype(BF16).astype(F32)
    for k, piece in enumerate((top, middle, decay - top - middle)):
        at = slice(half * (LANES + k), half * (LANES + k + 1))
        keep_ref[at, :] = jnp.where(side == 0, piece[0:half], piece[half:]).astype(BF16)
        offer_ref[at, :] = jnp.where(side == 0, piece[half:], piece[0:half]).astype(BF16)


def fetch(arrived_ref, stride, part, dims, wide_ref, small_ref, sems):
    start = dims[4] * stride
    wide = pltpu.make_async_copy(
        arrived_ref.at[:, part * stride : (part + 1) * stride], wide_ref, sems.at[0]
    )
    small = pltpu.make_async_copy(
        arrived_ref.at[:, start : start + small_ref.shape[1]], small_ref, sems.at[1]
    )
    small.start()
    wide.start()
    small.wait()
    return wide


def first_kernel(
    dims,
    place_ref,
    lengths_ref,
    arrived_ref,
    bias_ref,
    rate_ref,
    q_ref,
    rows_ref,
    columns_ref,
    decay_ref,
    x_ref,
    bc_ref,
    keep_ref,
    offer_ref,
    wide_ref,
    small_ref,
    sems,
):
    _, _, block_rows, over, groups, _, heads = dims
    slots = arrived_ref.shape[0]
    wide = fetch(arrived_ref, wide_ref.shape[1], 0, dims, wide_ref, small_ref, sems)
    meta = small_ref[:, 2 * groups * LANES : (2 * groups + 1) * LANES]
    turned = meta.astype(F32).T
    target = iota((block_rows, slots), 0) + 1
    own = onehot(target == turned[heads : heads + 1, :].astype(jnp.int32))
    raw = dot(own, meta).T[0:heads, :]
    if over:
        half = ROWS // 2
        inside = iota((1, slots), 1) % ROWS
        spot = jnp.where(inside < half, turned[LANES // 2 + heads : LANES // 2 + heads + 1, :], 0.0)
        low = onehot(target == spot.astype(jnp.int32))
        high = onehot(target == pltpu.roll(spot, half, 1).astype(jnp.int32))
        q_ref[:, 0:slots] = low
        q_ref[:, slots : 2 * slots] = own
        q_ref[:, 2 * slots :] = high
        raw = raw + dot(low, meta).T[LANES // 2 : LANES // 2 + heads, :]
    else:
        q_ref[...] = own
    raw = raw + column_of(bias_ref[...])
    step = jnp.maximum(raw, 0.0) + jnp.log1p(jnp.exp(-jnp.abs(raw)))
    logs = -step * jnp.exp(column_of(rate_ref[...]))
    upper = jnp.where(
        iota((block_rows, block_rows), 0) <= iota((block_rows, block_rows), 1), 1.0, 0.0
    )
    cum = jnp.dot(logs, upper, preferred_element_type=F32, precision=lax.Precision.HIGHEST)
    start = place_ref[0] * block_rows
    docs = doc_counts(lengths_ref, start + iota((1, block_rows), 1))
    last = doc_counts(lengths_ref, start + block_rows - 1 + jnp.zeros((1, 1), jnp.int32))
    before = doc_counts(lengths_ref, start - 1 + jnp.zeros((1, 1), jnp.int32))
    end = cum[:, block_rows - 1 : block_rows]
    entry = jnp.where(docs == before, jnp.exp(cum), 0.0)
    rows_ref[0] = step
    rows_ref[1] = cum
    rows_ref[2] = jnp.where(docs == last, jnp.exp(end - cum), 0.0) * step
    blank = jnp.zeros((LANES - heads, block_rows), F32)
    columns_ref[0] = jnp.concatenate([cum, blank], axis=0).T
    columns_ref[1] = jnp.concatenate([entry, blank], axis=0).T
    decay_ref[...] = jnp.broadcast_to(entry[:, block_rows - 1 : block_rows], decay_ref.shape)
    wide.wait()
    refs = (x_ref, bc_ref, keep_ref, offer_ref)
    land(dims, 0, place_ref[0] % 2, q_ref, wide_ref, small_ref, rows_ref, decay_ref, refs)


def later_kernel(
    dims,
    part,
    place_ref,
    arrived_ref,
    q_ref,
    rows_ref,
    decay_ref,
    x_ref,
    bc_ref,
    keep_ref,
    offer_ref,
    wide_ref,
    small_ref,
    sems,
):
    fetch(arrived_ref, wide_ref.shape[1], part, dims, wide_ref, small_ref, sems).wait()
    refs = (x_ref, bc_ref, keep_ref, offer_ref)
    land(dims, part, place_ref[0] % 2, q_ref, wide_ref, small_ref, rows_ref, decay_ref, refs)


def intra_kernel(groups, place_ref, lengths_ref, skip_ref, rows_ref, columns_ref, *refs):
    y_ref = refs[-1]
    block_rows, width = refs[0].shape
    per_group = width // LANES
    start = place_ref[0] * block_rows
    square = (block_rows, block_rows)
    row_docs = doc_counts(lengths_ref, start + iota((1, block_rows), 1))
    column_docs = doc_counts(lengths_ref, start + iota((block_rows, 1), 0))
    keep = (iota(square, 0) >= iota(square, 1)) & (row_docs == column_docs)
    for part in range(groups):
        x_ref, bc_ref = refs[2 * part : 2 * part + 2]
        scores = lax.dot_general(
            bc_ref[1], bc_ref[0], (((1,), (1,)), ((), ())), preferred_element_type=F32
        )
        for h in range(per_group):
            head = part * per_group + h
            across = columns_ref[0, :, head : head + 1] - rows_ref[1, head : head + 1, :]
            decay = jnp.exp(jnp.where(keep, across, -jnp.inf))
            weights = (scores * decay * rows_ref[0, head : head + 1, :]).astype(BF16)
            x_head = x_ref[:, h * LANES : (h + 1) * LANES]
            y_ref[:, head * LANES : (head + 1) * LANES] = dot(weights, x_head) + skip_ref[
                head
            ] * x_head.astype(F32)


def enter(place, keep, offer):
    blocks = lax.axis_size("ctx")
    half = keep.shape[0] // (LANES + 3)
    pairs = [(i, i ^ 1) for i in range(blocks)]
    even = place % 2 == 0

    def parts(values):
        state = values[: half * LANES].reshape(half, LANES, LANES).astype(F32)
        decay = values[half * LANES :].reshape(3, half, 1, LANES).astype(F32)
        return state, decay[0] + decay[1] + decay[2]

    got = lax.ppermute(offer, "ctx", pairs)
    own_state, own_decay = parts(keep)
    got_state, got_decay = parts(got)
    first = jnp.where(even, own_state, got_state)
    first_decay = jnp.where(even, own_decay, got_decay)
    second = jnp.where(even, got_state, own_state)
    second_decay = jnp.where(even, got_decay, own_decay)
    total = second_decay * first + second
    decay = own_decay * got_decay
    sent = total.astype(BF16)
    entering = jnp.zeros_like(total)
    for k in range(blocks // 2 - 1):
        hops = [(2 * k + side, 2 * k + 2 + side) for side in range(2)]
        come = lax.ppermute(sent, "ctx", hops).astype(F32)
        sent = (decay * come + total).astype(BF16)
        entering = entering + come
    after = first_decay * entering + first
    kept = jnp.where(even, entering, after).astype(BF16)
    other = jnp.where(even, after, entering).astype(BF16)
    other = lax.ppermute(other, "ctx", pairs)
    return kept.reshape(half * LANES, LANES), other.reshape(half * LANES, LANES)


def final_kernel(over, groups, place_ref, arrived_ref, q_ref, columns_ref, y_ref, gain_ref, *refs):
    out_ref, gated_ref = refs[-2:]
    block_rows, width = out_ref.shape
    per_group = width // LANES
    side = place_ref[0] % 2

    def one(part):
        bc_ref, keep_ref, got_ref = refs[3 * part : 3 * part + 3]
        first, second = placed(q_ref, arrived_ref, over, width)
        gated_ref[:, 0 : width // 2] = first
        gated_ref[:, width // 2 :] = second
        c_rows = bc_ref[0]
        squares = jnp.zeros((block_rows, LANES), F32)
        for h in range(per_group):
            head = part * per_group + h
            at = slice(h * LANES, (h + 1) * LANES)
            low = h < per_group // 2
            of = slice((h % (per_group // 2)) * LANES, (h % (per_group // 2) + 1) * LANES)
            state = jnp.where((side == 0) == low, keep_ref[of, :], got_ref[of, :])
            cross = dot(c_rows, state)
            value = y_ref[:, at] + columns_ref[0, :, head : head + 1] * cross
            gate = 0.5 * gated_ref[:, at]
            value = value * (gate * jnp.tanh(gate) + gate)
            gated_ref[:, at] = value
            squares = squares + value * value
        mean = jnp.sum(squares, axis=1, keepdims=True) * (1.0 / width)
        scale = lax.rsqrt(mean + 1e-05)
        for h in range(per_group):
            at = slice(h * LANES, (h + 1) * LANES)
            out_ref[:, at] = (gated_ref[:, at] * scale * gain_ref[:, at].astype(F32)).astype(BF16)

    for part in range(groups):
        pl.when(pl.program_id(0) == part)(functools.partial(one, part))


def shape(*dims, dtype=BF16):
    return jax.ShapeDtypeStruct(dims, dtype)


def body(
    x_load,
    z_load,
    b_load,
    c_load,
    dt_load,
    dt_bias,
    a_log,
    skip_gain,
    norm_gain,
    doc_lengths,
    anchor,
):
    load_rows = anchor.shape[0]
    owners = lax.axis_size("ctx")
    columns = lax.axis_size("head")
    block_rows = load_rows * columns
    capacity = 3 * load_rows // (2 * owners)
    heads = dt_bias.shape[0]
    groups = b_load.shape[1] // (columns * LANES)
    per_group = heads // groups
    width = per_group * LANES
    over = capacity > ROWS
    dims = (owners, columns, block_rows, over, groups, width, heads)
    slots = owners * columns * ROWS
    finds = 3 if over else 1
    anchor = anchor.reshape(1, load_rows)
    number = lax.axis_index("ctx").astype(jnp.int32)
    place = number.reshape(1)

    sent = pack(anchor, x_load, (b_load, c_load, dt_load), dims)
    arrived_x = exchange(sent, BOTH).reshape(slots, sent.shape[2])
    sent_z = pack(anchor, z_load, (), dims)
    arrived_z = exchange(sent_z, BOTH).reshape(slots, sent_z.shape[2])

    stride = width * 3 // 2 if over else width
    carried = (per_group // 2) * (LANES + 3)
    per_part = (
        shape(block_rows, width),
        shape(2, block_rows, LANES),
        shape(carried, LANES),
        shape(carried, LANES),
    )
    scratch = [
        pltpu.VMEM((slots, stride), BF16),
        pltpu.VMEM((slots, arrived_x.shape[1] - groups * stride), BF16),
        pltpu.SemaphoreType.DMA((2,)),
    ]
    anywhere = pl.BlockSpec(memory_space=pl.ANY)
    blocks, states = [], []
    for part in range(groups):
        if part == 0:
            finder, rows, turned, decay, x_block, both, keep, offer = pl.pallas_call(
                functools.partial(first_kernel, dims),
                in_specs=[SMEM, SMEM, anywhere, VMEM, VMEM],
                out_specs=[VMEM] * 8,
                out_shape=(
                    shape(block_rows, finds * slots),
                    shape(3, heads, block_rows, dtype=F32),
                    shape(2, block_rows, LANES, dtype=F32),
                    shape(heads, LANES, dtype=F32),
                )
                + per_part,
                scratch_shapes=scratch,
                compiler_params=PARAMS,
                name="land_first",
            )(
                place,
                doc_lengths,
                arrived_x,
                dt_bias.reshape(1, heads),
                a_log.reshape(1, heads),
            )
        else:
            x_block, both, keep, offer = pl.pallas_call(
                functools.partial(later_kernel, dims, part),
                in_specs=[SMEM, anywhere, VMEM, VMEM, VMEM],
                out_specs=[VMEM] * 4,
                out_shape=per_part,
                scratch_shapes=scratch,
                compiler_params=PARAMS,
                name="land_later",
            )(place, arrived_x, finder, rows, decay)
        blocks += [x_block, both]
        states.append(enter(number, keep, offer))
    y = pl.pallas_call(
        functools.partial(intra_kernel, groups),
        in_specs=[SMEM, SMEM, SMEM] + [VMEM] * (2 + len(blocks)),
        out_specs=VMEM,
        out_shape=shape(block_rows, groups * width, dtype=F32),
        compiler_params=PARAMS,
        name="intra",
    )(place, doc_lengths, skip_gain, rows, turned, *blocks)

    full = lambda a: pl.BlockSpec(a.shape, lambda i, n=a.ndim: (0,) * n)
    second = pl.BlockSpec((1, block_rows, LANES), lambda i: (1, 0, 0))
    in_specs = [
        SMEM,
        pl.BlockSpec((slots, stride), lambda i: (0, i)),
        full(finder),
        second,
        pl.BlockSpec((block_rows, width), lambda i: (0, i)),
        pl.BlockSpec((1, width), lambda i: (0, i)),
    ]
    operands = []
    for part in range(groups):
        operands += [blocks[2 * part + 1], *states[part]]
        in_specs += [second, full(states[part][0]), full(states[part][1])]
    return pl.pallas_call(
        functools.partial(final_kernel, over, groups),
        grid=(groups,),
        in_specs=in_specs,
        out_specs=pl.BlockSpec((block_rows, width), lambda i: (0, i)),
        out_shape=shape(block_rows, groups * width),
        scratch_shapes=[pltpu.VMEM((block_rows, width), F32)],
        compiler_params=PARAMS,
        name="final",
    )(place, arrived_z, finder, turned, y, norm_gain.reshape(1, groups * width), *operands)


def solution(mesh):
    in_specs = (
        P(BOTH, None),
        P(BOTH, None),
        P(BOTH, None),
        P(BOTH, None),
        P(BOTH, None),
        P("head"),
        P("head"),
        P("head"),
        P("head"),
        P(),
        P(BOTH),
    )
    out_specs = P("ctx", "head")

    return jax.shard_map(body, mesh=mesh, in_specs=in_specs, out_specs=out_specs, check_vma=False)
```

```python
import functools

import jax
import jax.numpy as jnp
from jax import lax
from jax.experimental import pallas as pl
from jax.experimental.pallas import tpu as pltpu
from jax.sharding import PartitionSpec as P

LANES = 128
ROWS = 8
F32 = jnp.float32
BF16 = jnp.bfloat16
BOTH = ("ctx", "head")
VMEM = pl.BlockSpec(memory_space=pltpu.VMEM)
SMEM = pl.BlockSpec(memory_space=pltpu.SMEM)
PARAMS = pltpu.CompilerParams(vmem_limit_bytes=56 * 1024 * 1024)


def iota(shape, dim):
    return lax.broadcasted_iota(jnp.int32, shape, dim)


def dot(left, right):
    return jnp.dot(left, right, preferred_element_type=F32)


def onehot(mask):
    return jnp.where(mask, 1.0, 0.0).astype(BF16)


def send_onehots(anchor, turn, owners, block_rows, over):
    rows = anchor.shape[1]
    owner = jnp.zeros_like(anchor)
    for k in range(1, owners):
        owner = owner + jnp.where(anchor >= k * block_rows, 1, 0)
    eye = iota((rows, rows), 0) == iota((rows, rows), 1)
    owner_f = owner.astype(F32)
    owner_col = jnp.sum(jnp.where(eye, owner_f, 0.0), axis=1, keepdims=True)
    earlier = (owner_col == owner_f) & (iota((rows, rows), 0) < iota((rows, rows), 1))
    rank = jnp.sum(jnp.where(earlier, 1.0, 0.0), axis=0, keepdims=True).astype(jnp.int32)
    place = (anchor - owner * block_rows + 1).astype(F32)
    place_col = jnp.sum(jnp.where(eye, place, 0.0), axis=1, keepdims=True)
    slot = iota((owners * ROWS, rows), 0)
    first = (owner ^ turn) * ROWS + rank
    base = onehot((slot == first) & (rank < ROWS))
    if not over:
        return base, None, None, place_col
    low = onehot((slot == first - ROWS) & (rank >= ROWS))
    high = onehot((slot == first - ROWS // 2) & (rank >= ROWS))
    return base, low, high, place_col


def pack_kernel(dims, small, *refs):
    owners, _, block_rows, over, groups, width, heads = dims
    place_ref = None if small else refs[0]
    anchor_ref, wide_ref, *refs = refs if small else refs[1:]
    out_ref, base_ref, extra_ref, spot_ref = refs[-4:]
    load_rows = wide_ref.shape[0]

    @pl.when(pl.program_id(0) == 0)
    def _():
        turn = jnp.int32(0) if small else place_ref[0]
        base, low, high, place_col = send_onehots(anchor_ref[...], turn, owners, block_rows, over)
        base_ref[...] = base
        spot_ref[...] = jnp.broadcast_to(place_col, spot_ref.shape)
        if over:
            extra_ref[:, 0:load_rows] = low
            extra_ref[:, load_rows:] = high

    def put(column, values):
        values = values.astype(BF16).reshape(owners, ROWS, values.shape[1])
        to = slice(column, column + values.shape[2])
        if small:
            out_ref[:, 0, :, to] = values
        else:
            out_ref[0, :, :, to] = values

    def folded(low, high):
        return dot(extra_ref[...], jnp.concatenate([low, high], axis=0))

    column = 0
    for part in range(groups):
        at = part * width
        put(column, dot(base_ref[...], wide_ref[:, at : at + width]))
        column += width
        if over:
            half = width // 2
            put(column, folded(wide_ref[:, at : at + half], wide_ref[:, at + half : at + width]))
            column += half
    if not small:
        return
    b_part, c_part, dt_part = refs[0][...], refs[1][...], refs[2][...]
    steps = dt_part.astype(F32)
    own = jnp.zeros_like(steps)
    lane = iota(steps.shape, 1)
    for k in range(LANES // heads):
        shifted = steps if k == 0 else pltpu.roll(steps, LANES - k * heads, 1)
        own = own + jnp.where(pl.program_id(0) == k, shifted, 0.0)
    meta = jnp.where(lane < heads, own, jnp.where(lane == heads, spot_ref[...], 0.0))
    put(column, dot(base_ref[...], jnp.concatenate([b_part, c_part], axis=1)))
    column += 2 * b_part.shape[1]
    tile = dot(base_ref[...], meta.astype(BF16))
    if over:
        turned = pltpu.roll(meta, LANES // 2, 1).astype(BF16)
        tile = tile + dot(extra_ref[:, 0:load_rows], turned)
    put(column, tile)
    if over:
        put(column + LANES, folded(b_part, c_part))


def pack(place, anchor, wide, smalls, dims):
    owners, columns, _, over, groups, width, _ = dims
    load_rows = wide.shape[0]
    total = groups * (width * 3 // 2 if over else width)
    if smalls:
        total += LANES * (groups * (3 if over else 2) + 1)
        grouped, block, index = (owners, columns), (owners, 1), lambda i, *p: (0, i, 0, 0)
        column = lambda i, *p: (0, i)
    else:
        grouped, block, index = (columns, owners), (1, owners), lambda i, p: (i, 0, 0, 0)
        column = lambda i, p: (0, i ^ p[1])
    in_specs = [
        pl.BlockSpec((1, load_rows), lambda i, *p: (0, 0)),
        pl.BlockSpec((load_rows, groups * width), column),
    ]
    if smalls:
        in_specs += [pl.BlockSpec((load_rows, groups * LANES), column)] * 2
        in_specs += [pl.BlockSpec((load_rows, LANES), lambda i, *p: (0, 0))]
    return pl.pallas_call(
        functools.partial(pack_kernel, dims, bool(smalls)),
        grid_spec=pltpu.PrefetchScalarGridSpec(
            num_scalar_prefetch=len(place),
            grid=(columns,),
            in_specs=in_specs,
            out_specs=pl.BlockSpec(block + (ROWS, total), index),
            scratch_shapes=[
                pltpu.VMEM((owners * ROWS, load_rows), BF16),
                pltpu.VMEM((owners * ROWS, 2 * load_rows), BF16),
                pltpu.VMEM((load_rows, LANES), F32),
            ],
        ),
        out_shape=shape(*grouped, ROWS, total),
        compiler_params=PARAMS,
        name="pack",
    )(*place, anchor, wide, *smalls)


def exchange(values, axes):
    return lax.all_to_all(values, axes, split_axis=0, concat_axis=0, tiled=True)


def doc_counts(lengths_ref, positions):
    count = jnp.zeros_like(positions)
    start = jnp.int32(0)
    for k in range(lengths_ref.shape[0]):
        count = count + jnp.where(positions >= start, 1, 0)
        start = start + lengths_ref[k]
    return count


def column_of(row):
    size = row.shape[1]
    eye = iota((size, size), 0) == iota((size, size), 1)
    return jnp.sum(jnp.where(eye, row, 0.0), axis=1, keepdims=True)


def placed(q_ref, values_refs, over, width):
    slots = sum(ref.shape[0] for ref in values_refs)
    half = width // 2

    def part(k):
        pieces = [ref[:, k * half : (k + 1) * half] for ref in values_refs]
        return pieces[0] if len(pieces) == 1 else jnp.concatenate(pieces, axis=0)

    if not over:
        return dot(q_ref[...], part(0)), dot(q_ref[...], part(1))
    extra = part(2)
    first = jnp.concatenate([extra, part(0)], axis=0)
    second = jnp.concatenate([part(1), extra], axis=0)
    return dot(q_ref[:, 0 : 2 * slots], first), dot(q_ref[:, slots : 3 * slots], second)


def find(q_ref, meta, block_rows, over, heads):
    slots = meta.shape[0]
    turned = meta.T
    target = iota((block_rows, slots), 0) + 1
    own = onehot(target == turned[heads : heads + 1, :].astype(jnp.int32))
    if not over:
        q_ref[...] = own
        return
    half = ROWS // 2
    inside = iota((1, slots), 1) % ROWS
    spot = jnp.where(inside < half, turned[LANES // 2 + heads : LANES // 2 + heads + 1, :], 0.0)
    q_ref[:, 0:slots] = onehot(target == spot.astype(jnp.int32))
    q_ref[:, slots : 2 * slots] = own
    q_ref[:, 2 * slots :] = onehot(target == pltpu.roll(spot, half, 1).astype(jnp.int32))


def land(dims, part, side, q_ref, wide_ref, small_ref, rows_ref, decay_ref, refs):
    _, _, _, over, groups, width, _ = dims
    x_ref, bc_ref, keep_ref, offer_ref = refs
    slots = wide_ref.shape[0]
    per_group = width // LANES
    b_slots = small_ref[:, part * LANES : (part + 1) * LANES]
    c_slots = small_ref[:, (groups + part) * LANES : (groups + part + 1) * LANES]
    if over:
        at = (2 * groups + 1 + part) * LANES
        extra = small_ref[:, at : at + LANES]
        b_all = dot(q_ref[:, 0 : 2 * slots], jnp.concatenate([extra, b_slots], axis=0))
        c_all = dot(q_ref[:, slots : 3 * slots], jnp.concatenate([c_slots, extra], axis=0))
    else:
        b_all = dot(q_ref[...], b_slots)
        c_all = dot(q_ref[...], c_slots)
    bc_ref[0] = b_all.astype(BF16)
    bc_ref[1] = c_all.astype(BF16)
    first, second = placed(q_ref, [wide_ref], over, width)
    x_ref[:, 0 : width // 2] = first.astype(BF16)
    x_ref[:, width // 2 :] = second.astype(BF16)
    b_turned = b_all.T

    def state_of(h):
        head = part * per_group + h
        weighted = (b_turned * rows_ref[2, head : head + 1, :]).astype(BF16)
        return dot(weighted, x_ref[:, h * LANES : (h + 1) * LANES])

    half = per_group // 2
    for q in range(half):
        low, high = state_of(q), state_of(half + q)
        at = slice(q * LANES, (q + 1) * LANES)
        keep_ref[at, :] = jnp.where(side == 0, low, high).astype(BF16)
        offer_ref[at, :] = jnp.where(side == 0, high, low).astype(BF16)
    decay = decay_ref[part * per_group : (part + 1) * per_group, :]
    top = decay.astype(BF16).astype(F32)
    middle = (decay - top).astype(BF16).astype(F32)
    for k, piece in enumerate((top, middle, decay - top - middle)):
        at = slice(half * (LANES + k), half * (LANES + k + 1))
        keep_ref[at, :] = jnp.where(side == 0, piece[0:half], piece[half:]).astype(BF16)
        offer_ref[at, :] = jnp.where(side == 0, piece[half:], piece[0:half]).astype(BF16)


def fetch(arrived_ref, stride, part, dims, wide_ref, small_ref, sems):
    start = dims[4] * stride
    wide = pltpu.make_async_copy(
        arrived_ref.at[:, part * stride : (part + 1) * stride], wide_ref, sems.at[0]
    )
    small = pltpu.make_async_copy(
        arrived_ref.at[:, start : start + small_ref.shape[1]], small_ref, sems.at[1]
    )
    small.start()
    wide.start()
    small.wait()
    return wide


def first_kernel(
    dims,
    place_ref,
    lengths_ref,
    arrived_ref,
    bias_ref,
    rate_ref,
    q_ref,
    turned_q_ref,
    rows_ref,
    columns_ref,
    decay_ref,
    x_ref,
    bc_ref,
    keep_ref,
    offer_ref,
    wide_ref,
    small_ref,
    meta_ref,
    sems,
):
    owners, columns, block_rows, over, groups, _, heads = dims
    slots = arrived_ref.shape[0]
    wide = fetch(arrived_ref, wide_ref.shape[1], 0, dims, wide_ref, small_ref, sems)
    meta = small_ref[:, 2 * groups * LANES : (2 * groups + 1) * LANES]
    meta_ref[0] = meta.astype(F32)
    find(q_ref, meta_ref[0], block_rows, over, heads)

    def move(i, carry):
        loader = (place_ref[0] ^ (i // columns)) * columns + (place_ref[1] ^ (i % columns))
        to = pl.multiple_of(i * ROWS, ROWS)
        meta_ref[1, pl.ds(to, ROWS), :] = meta_ref[0, pl.ds(pl.multiple_of(loader * ROWS, ROWS), ROWS), :]
        return carry

    lax.fori_loop(0, owners * columns, move, 0)
    find(turned_q_ref, meta_ref[1], block_rows, over, heads)
    if over:
        raw = dot(q_ref[:, slots : 2 * slots], meta).T[0:heads, :]
        raw = raw + dot(q_ref[:, 0:slots], meta).T[LANES // 2 : LANES // 2 + heads, :]
    else:
        raw = dot(q_ref[...], meta).T[0:heads, :]
    raw = raw + column_of(bias_ref[...])
    step = jnp.maximum(raw, 0.0) + jnp.log1p(jnp.exp(-jnp.abs(raw)))
    logs = -step * jnp.exp(column_of(rate_ref[...]))
    upper = jnp.where(
        iota((block_rows, block_rows), 0) <= iota((block_rows, block_rows), 1), 1.0, 0.0
    )
    cum = jnp.dot(logs, upper, preferred_element_type=F32, precision=lax.Precision.HIGHEST)
    start = place_ref[0] * block_rows
    docs = doc_counts(lengths_ref, start + iota((1, block_rows), 1))
    last = doc_counts(lengths_ref, start + block_rows - 1 + jnp.zeros((1, 1), jnp.int32))
    before = doc_counts(lengths_ref, start - 1 + jnp.zeros((1, 1), jnp.int32))
    end = cum[:, block_rows - 1 : block_rows]
    entry = jnp.where(docs == before, jnp.exp(cum), 0.0)
    rows_ref[0] = step
    rows_ref[1] = cum
    rows_ref[2] = jnp.where(docs == last, jnp.exp(end - cum), 0.0) * step
    blank = jnp.zeros((LANES - heads, block_rows), F32)
    columns_ref[0] = jnp.concatenate([cum, blank], axis=0).T
    columns_ref[1] = jnp.concatenate([entry, blank], axis=0).T
    decay_ref[...] = jnp.broadcast_to(entry[:, block_rows - 1 : block_rows], decay_ref.shape)
    wide.wait()
    refs = (x_ref, bc_ref, keep_ref, offer_ref)
    land(dims, 0, place_ref[0] % 2, q_ref, wide_ref, small_ref, rows_ref, decay_ref, refs)


def later_kernel(
    dims,
    part,
    place_ref,
    arrived_ref,
    q_ref,
    rows_ref,
    decay_ref,
    x_ref,
    bc_ref,
    keep_ref,
    offer_ref,
    wide_ref,
    small_ref,
    sems,
):
    fetch(arrived_ref, wide_ref.shape[1], part, dims, wide_ref, small_ref, sems).wait()
    refs = (x_ref, bc_ref, keep_ref, offer_ref)
    land(dims, part, place_ref[0] % 2, q_ref, wide_ref, small_ref, rows_ref, decay_ref, refs)


def intra_kernel(groups, place_ref, lengths_ref, skip_ref, rows_ref, columns_ref, *refs):
    y_ref = refs[-1]
    block_rows, width = refs[0].shape
    per_group = width // LANES
    start = place_ref[0] * block_rows
    square = (block_rows, block_rows)
    row_docs = doc_counts(lengths_ref, start + iota((1, block_rows), 1))
    column_docs = doc_counts(lengths_ref, start + iota((block_rows, 1), 0))
    keep = (iota(square, 0) >= iota(square, 1)) & (row_docs == column_docs)
    for part in range(groups):
        x_ref, bc_ref = refs[2 * part : 2 * part + 2]
        scores = lax.dot_general(
            bc_ref[1], bc_ref[0], (((1,), (1,)), ((), ())), preferred_element_type=F32
        )
        for h in range(per_group):
            head = part * per_group + h
            across = columns_ref[0, :, head : head + 1] - rows_ref[1, head : head + 1, :]
            decay = jnp.exp(jnp.where(keep, across, -jnp.inf))
            weights = (scores * decay * rows_ref[0, head : head + 1, :]).astype(BF16)
            x_head = x_ref[:, h * LANES : (h + 1) * LANES]
            y_ref[:, head * LANES : (head + 1) * LANES] = dot(weights, x_head) + skip_ref[
                head
            ] * x_head.astype(F32)


def enter(place, keep, offer):
    blocks = lax.axis_size("ctx")
    half = keep.shape[0] // (LANES + 3)
    pairs = [(i, i ^ 1) for i in range(blocks)]
    even = place % 2 == 0

    def parts(values):
        state = values[: half * LANES].reshape(half, LANES, LANES).astype(F32)
        decay = values[half * LANES :].reshape(3, half, 1, LANES).astype(F32)
        return state, decay[0] + decay[1] + decay[2]

    got = lax.ppermute(offer, "ctx", pairs)
    own_state, own_decay = parts(keep)
    got_state, got_decay = parts(got)
    first = jnp.where(even, own_state, got_state)
    first_decay = jnp.where(even, own_decay, got_decay)
    second = jnp.where(even, got_state, own_state)
    second_decay = jnp.where(even, got_decay, own_decay)
    total = second_decay * first + second
    decay = own_decay * got_decay
    sent = total.astype(BF16)
    entering = jnp.zeros_like(total)
    for k in range(blocks // 2 - 1):
        hops = [(2 * k + side, 2 * k + 2 + side) for side in range(2)]
        come = lax.ppermute(sent, "ctx", hops).astype(F32)
        sent = (decay * come + total).astype(BF16)
        entering = entering + come
    after = first_decay * entering + first
    kept = jnp.where(even, entering, after).astype(BF16)
    other = jnp.where(even, after, entering).astype(BF16)
    other = lax.ppermute(other, "ctx", pairs)
    return kept.reshape(half * LANES, LANES), other.reshape(half * LANES, LANES)


def final_kernel(over, groups, place_ref, q_ref, columns_ref, y_ref, gain_ref, *refs):
    arrived_refs = refs[3 * groups : -2]
    out_ref, gated_ref = refs[-2:]
    block_rows, width = out_ref.shape
    per_group = width // LANES
    side = place_ref[0] % 2

    def one(part):
        bc_ref, keep_ref, got_ref = refs[3 * part : 3 * part + 3]
        first, second = placed(q_ref, arrived_refs, over, width)
        gated_ref[:, 0 : width // 2] = first
        gated_ref[:, width // 2 :] = second
        c_rows = bc_ref[0]
        squares = jnp.zeros((block_rows, LANES), F32)
        for h in range(per_group):
            head = part * per_group + h
            at = slice(h * LANES, (h + 1) * LANES)
            low = h < per_group // 2
            of = slice((h % (per_group // 2)) * LANES, (h % (per_group // 2) + 1) * LANES)
            state = jnp.where((side == 0) == low, keep_ref[of, :], got_ref[of, :])
            cross = dot(c_rows, state)
            value = y_ref[:, at] + columns_ref[0, :, head : head + 1] * cross
            gate = 0.5 * gated_ref[:, at]
            value = value * (gate * jnp.tanh(gate) + gate)
            gated_ref[:, at] = value
            squares = squares + value * value
        mean = jnp.sum(squares, axis=1, keepdims=True) * (1.0 / width)
        scale = lax.rsqrt(mean + 1e-05)
        for h in range(per_group):
            at = slice(h * LANES, (h + 1) * LANES)
            out_ref[:, at] = (gated_ref[:, at] * scale * gain_ref[:, at].astype(F32)).astype(BF16)

    for part in range(groups):
        pl.when(pl.program_id(0) == part)(functools.partial(one, part))


def shape(*dims, dtype=BF16):
    return jax.ShapeDtypeStruct(dims, dtype)


def body(
    x_load,
    z_load,
    b_load,
    c_load,
    dt_load,
    dt_bias,
    a_log,
    skip_gain,
    norm_gain,
    doc_lengths,
    anchor,
):
    load_rows = anchor.shape[0]
    owners = lax.axis_size("ctx")
    columns = lax.axis_size("head")
    block_rows = load_rows * columns
    capacity = 3 * load_rows // (2 * owners)
    heads = dt_bias.shape[0]
    groups = b_load.shape[1] // (columns * LANES)
    per_group = heads // groups
    width = per_group * LANES
    over = capacity > ROWS
    dims = (owners, columns, block_rows, over, groups, width, heads)
    slots = owners * columns * ROWS
    finds = 3 if over else 1
    anchor = anchor.reshape(1, load_rows)
    number = lax.axis_index("ctx").astype(jnp.int32)
    place = jnp.stack([number, lax.axis_index("head").astype(jnp.int32)])

    sent = pack((), anchor, x_load, (b_load, c_load, dt_load), dims)
    sent = sent.reshape(owners * columns, ROWS, sent.shape[3])
    arrived_x = exchange(sent, BOTH).reshape(slots, sent.shape[2])
    sent_z = pack((place,), anchor, z_load, (), dims)
    gathered = [sent_z[0]]
    for k in range(1, columns):
        hops = [(i, i ^ k) for i in range(columns)]
        gathered.append(lax.ppermute(sent_z[k], "head", hops))
    arrived_z = []
    for k in range(owners):
        piece = jnp.concatenate([a[k] for a in gathered], axis=0)
        if k > 0:
            piece = lax.ppermute(piece, "ctx", [(i, i ^ k) for i in range(owners)])
        arrived_z.append(piece)

    stride = width * 3 // 2 if over else width
    carried = (per_group // 2) * (LANES + 3)
    per_part = (
        shape(block_rows, width),
        shape(2, block_rows, LANES),
        shape(carried, LANES),
        shape(carried, LANES),
    )
    scratch = [
        pltpu.VMEM((slots, stride), BF16),
        pltpu.VMEM((slots, arrived_x.shape[1] - groups * stride), BF16),
        pltpu.SemaphoreType.DMA((2,)),
    ]
    anywhere = pl.BlockSpec(memory_space=pl.ANY)
    blocks, states = [], []
    for part in range(groups):
        if part == 0:
            (finder, finder_z, rows, turned, decay, x_block, both, keep, offer) = pl.pallas_call(
                functools.partial(first_kernel, dims),
                in_specs=[SMEM, SMEM, anywhere, VMEM, VMEM],
                out_specs=[VMEM] * 9,
                out_shape=(
                    shape(block_rows, finds * slots),
                    shape(block_rows, finds * slots),
                    shape(3, heads, block_rows, dtype=F32),
                    shape(2, block_rows, LANES, dtype=F32),
                    shape(heads, LANES, dtype=F32),
                )
                + per_part,
                scratch_shapes=scratch[:2] + [pltpu.VMEM((2, slots, LANES), F32)] + scratch[2:],
                compiler_params=PARAMS,
                name="land_first",
            )(
                place,
                doc_lengths,
                arrived_x,
                dt_bias.reshape(1, heads),
                a_log.reshape(1, heads),
            )
        else:
            x_block, both, keep, offer = pl.pallas_call(
                functools.partial(later_kernel, dims, part),
                in_specs=[SMEM, anywhere, VMEM, VMEM, VMEM],
                out_specs=[VMEM] * 4,
                out_shape=per_part,
                scratch_shapes=scratch,
                compiler_params=PARAMS,
                name="land_later",
            )(place, arrived_x, finder, rows, decay)
        blocks += [x_block, both]
        states.append(enter(number, keep, offer))
    y = pl.pallas_call(
        functools.partial(intra_kernel, groups),
        in_specs=[SMEM, SMEM, SMEM] + [VMEM] * (2 + len(blocks)),
        out_specs=VMEM,
        out_shape=shape(block_rows, groups * width, dtype=F32),
        compiler_params=PARAMS,
        name="intra",
    )(place, doc_lengths, skip_gain, rows, turned, *blocks)

    full = lambda a: pl.BlockSpec(a.shape, lambda i, n=a.ndim: (0,) * n)
    second = pl.BlockSpec((1, block_rows, LANES), lambda i: (1, 0, 0))
    in_specs = [
        SMEM,
        full(finder_z),
        second,
        pl.BlockSpec((block_rows, width), lambda i: (0, i)),
        pl.BlockSpec((1, width), lambda i: (0, i)),
    ]
    operands = []
    for part in range(groups):
        operands += [blocks[2 * part + 1], *states[part]]
        in_specs += [second, full(states[part][0]), full(states[part][1])]
    for piece in arrived_z:
        operands.append(piece)
        in_specs.append(pl.BlockSpec((piece.shape[0], stride), lambda i: (0, i)))
    return pl.pallas_call(
        functools.partial(final_kernel, over, groups),
        grid=(groups,),
        in_specs=in_specs,
        out_specs=pl.BlockSpec((block_rows, width), lambda i: (0, i)),
        out_shape=shape(block_rows, groups * width),
        scratch_shapes=[pltpu.VMEM((block_rows, width), F32)],
        compiler_params=PARAMS,
        name="final",
    )(place, finder_z, turned, y, norm_gain.reshape(1, groups * width), *operands)


def solution(mesh):
    in_specs = (
        P(BOTH, None),
        P(BOTH, None),
        P(BOTH, None),
        P(BOTH, None),
        P(BOTH, None),
        P("head"),
        P("head"),
        P("head"),
        P("head"),
        P(),
        P(BOTH),
    )
    out_specs = P("ctx", "head")

    return jax.shard_map(body, mesh=mesh, in_specs=in_specs, out_specs=out_specs, check_vma=False)
```
